256 devices in a mesh: chan: 16 (over y_hi, z), strip: 16 (over y_lo, x, core).
Axes of the slice: x: 4, y: 4 (y_hi: 2, y_lo: 2; y = y_hi * 2 + y_lo), z: 8, core: 2. Of those that a mesh axis runs over, the one named last changes fastest.
Arguments:
- image: bfloat16 [256, 48, 1280], P('chan', 'strip'), may hold values from -6 to 6
- filter_one: bfloat16 [256, 9, 256], P('strip', None, 'chan'), may hold values from -0.125 to 0.125
- filter_two: bfloat16 [256, 9, 256], P('strip', None, 'chan'), may hold values from -0.125 to 0.125
- cotangent: bfloat16 [256, 48, 1280], P('chan', 'strip'), may hold values from -6 to 6
Outputs:
- image_grad: bfloat16 [256, 48, 1280], P('chan', 'strip')
- grad_one: float32 [256, 9, 256], P('strip', None, 'chan')
- grad_two: float32 [256, 9, 256], P('strip', None, 'chan')
The draws below stay inside these ranges and needn't reach their ends.
All inputs are finite; a program needn't handle non-finite values.
Results may differ from the reference program's by a relative error of at most 0.018.
Values may be sent and summed in bfloat16 or wider, within the bound.
No kernel may reach another device: no remote copies, remote signals or barrier semaphores. Data moves between devices by JAX's collectives and lax.ppermute only.
A program may use at most 64 MiB of HBM per device.

```python
import math
import jax
import jax.numpy as jnp

C = 256
COLS = 1280
ROWS = 48


def block_levels(own_key, extent, pieces, least, high):
    def one(axis_at, blocks):
        heights = jax.random.uniform(jax.random.fold_in(jax.random.fold_in(own_key, 6), axis_at), (blocks,), jnp.float32, least / len(pieces), high / len(pieces))
        return jnp.repeat(jnp.exp(heights), extent[axis_at] // blocks).reshape((-1,) + (1,) * (len(extent) - axis_at - 1))

    loudness = one(*pieces[0])
    for cut in pieces[1:]:
        loudness = loudness * one(*cut)
    return loudness


def scatter_about(stream_key, dims, spread, most, shards=(), kind=jnp.bfloat16):
    entries = spread * jax.random.normal(stream_key, dims, jnp.float32)
    if shards:
        entries = entries * block_levels(stream_key, dims, shards, -0.22, 0.18)
    return jnp.clip(entries, -most, most).astype(kind)


def setup_inputs(seed: int = 0) -> dict:
    keys = jax.random.split(jax.random.key(seed), 5)
    image = scatter_about(keys[0], (C, ROWS, COLS), 1.0, 6.0, ((0, 16), (1, 16)))
    filter_one = scatter_about(keys[1], (C, 9, C), (9 * C) ** -0.5, 0.125, ((0, 16), (2, 16)))
    filter_two = scatter_about(keys[2], (C, 9, C), (9 * C) ** -0.5, 0.125, ((0, 16), (2, 16)))
    cotangent = scatter_about(keys[3], (C, ROWS, COLS), 1.0, 6.0, ((0, 16), (1, 16)))
    return {"image": image, "filter_one": filter_one, "filter_two": filter_two, "cotangent": cotangent}


def silu_slope(values):
    sigma = jax.nn.sigmoid(values)
    return sigma * (1.0 + values * (1.0 - sigma))

def conv(values, filters):
    height, breadth = (values.shape[1], values.shape[2])
    padded = jnp.pad(values.astype(jnp.float32), ((0, 0), (2, 2), (2, 2)))
    weights = filters.astype(jnp.float32)
    result = jnp.zeros((filters.shape[2], height, breadth), jnp.float32)
    for row_tap in range(3):
        for col_tap in range(3):
            window = padded[:, 2 * row_tap:2 * row_tap + height, 2 * col_tap:2 * col_tap + breadth]
            result = result + jnp.einsum('chw,co->ohw', window, weights[:, 3 * row_tap + col_tap, :])
    return result

def back(grads, filters):
    height, breadth = (grads.shape[1], grads.shape[2])
    padded = jnp.pad(grads.astype(jnp.float32), ((0, 0), (2, 2), (2, 2)))
    weights = filters.astype(jnp.float32)
    result = jnp.zeros((filters.shape[0], height, breadth), jnp.float32)
    for row_tap in range(3):
        for col_tap in range(3):
            window = padded[:, 4 - 2 * row_tap:4 - 2 * row_tap + height, 4 - 2 * col_tap:4 - 2 * col_tap + breadth]
            result = result + jnp.einsum('ohw,co->chw', window, weights[:, 3 * row_tap + col_tap, :])
    return result

def filter_terms(values, grads):
    height, breadth = (grads.shape[1], grads.shape[2])
    padded = jnp.pad(values.astype(jnp.float32), ((0, 0), (2, 2), (2, 2)))
    grad_full = grads.astype(jnp.float32)
    blocks = []
    for row_tap in range(3):
        for col_tap in range(3):
            window = padded[:, 2 * row_tap:2 * row_tap + height, 2 * col_tap:2 * col_tap + breadth]
            blocks.append(jnp.einsum('chw,ohw->co', window, grad_full))
    return jnp.stack(blocks, axis=1)

def reference(image, filter_one, filter_two, cotangent):
    scale = 1.0 / math.sqrt(ROWS * COLS)
    first_pre = conv(image, filter_one)
    hidden = jax.nn.silu(first_pre).astype(jnp.bfloat16)
    second_pre = conv(hidden, filter_two)
    second_grad = (cotangent.astype(jnp.float32) * silu_slope(second_pre)).astype(jnp.bfloat16)
    hidden_grad = back(second_grad, filter_two)
    first_grad = (hidden_grad * silu_slope(first_pre)).astype(jnp.bfloat16)
    image_grad = back(first_grad, filter_one).astype(jnp.bfloat16)
    grad_two = filter_terms(hidden, second_grad) * scale
    grad_one = filter_terms(image, first_grad) * scale
    return (image_grad, grad_one, grad_two)
```

```python
import functools
import math

import jax
import jax.numpy as jnp
from jax import lax
from jax.experimental import pallas as pl
from jax.experimental.pallas import tpu as pltpu
from jax.sharding import Mesh
from jax.sharding import PartitionSpec as P

AXES = ("yh", "z", "yl", "x", "core")
CHAN = ("yh", "z")
STRIP = ("yl", "x", "core")
TORUS = ("yh", "yl", "x")
F32 = jnp.float32
BF16 = jnp.bfloat16

W = 32


def call(kernel, outs, scratch, args, prefetch):
    return pl.pallas_call(
        kernel,
        out_shape=outs,
        in_specs=[pl.BlockSpec(memory_space=pltpu.SMEM)]
        + [pl.BlockSpec(memory_space=pltpu.VMEM)] * len(args),
        out_specs=jax.tree.map(lambda _: pl.BlockSpec(memory_space=pltpu.VMEM), outs),
        scratch_shapes=scratch,
    )(prefetch, *args)


def shape(dims, kind=BF16):
    return jax.ShapeDtypeStruct(dims, kind)


def torus_at(y, x, d, sign):
    return ((y + sign * (d // 4) + 4) % 4) * 4 + (x + sign * (d % 4) + 4) % 4


def windows_kernel(at, image, cotangent, pieces, *rest):
    outs, (image_wide, cotangent_wide, windows) = rest[:8], rest[8:]
    for wide, source in ((image_wide, image), (cotangent_wide, cotangent)):
        wide[:, :256] = jnp.zeros((48, 256), F32)
        wide[:, 1536:] = jnp.zeros((48, 256), F32)
        wide[:, 256:1536] = source[...].astype(F32)
    lane = lax.broadcasted_iota(jnp.int32, (48, 384), 1)
    for z in range(8):
        first = 256 + 160 * z - 8
        base = first // 128 * 128
        left = pltpu.roll(image_wide[:, base : base + 384], 384 - (first - base), 1)
        second = 256 + 160 * z - 4 - 176
        base = second // 128 * 128
        right = pltpu.roll(cotangent_wide[:, base : base + 512], 512 - (second - base), 1)[:, :384]
        windows[z, :48, :] = jnp.where(lane < 176, left, right).astype(BF16)
        windows[z, 48:, :] = pieces[...]
    for d in range(8):
        outs[d][...] = windows[(at[1] + d) % 8]


def turn_kernel(at, *rest):
    pieces, outs, (held, turned, chunk, chunks) = rest[:8], rest[8:24], rest[24:]
    for d in range(8):
        held[(at[1] - d + 8) % 8] = pieces[d][...]
    for i in range(3):
        turned[...] = held[:, 16 * i : 16 * i + 16, :].reshape(128, 384).astype(F32).T
        for j in range(16):
            chunk[:32, :] = turned[10 * j : 10 * j + 32, :]
            chunk[26:48, :] = turned[176 + 10 * j : 198 + 10 * j, :]
            chunks[j, 48 * i : 48 * i + 48, :] = chunk[...].astype(BF16)
    filters = held[:, 48:, :].reshape(128, 384).astype(F32).T[:288].astype(BF16)
    for d in range(16):
        outs[d][:144, :] = chunks[torus_at(at[2], at[3], d, 1)]
        outs[d][144:, :] = filters


def sigmoid(v):
    return 1.0 / (1.0 + jnp.exp(-v))


def conv_kernel(at, *rest):
    own, other = rest[:16], rest[16:32]
    send, keep, image_send, image_keep = rest[32:36]
    acts, wide, pre, hidden, second, first, mine, terms, image_rows = rest[36:]
    y, x, core, z = at[2], at[3], at[4], at[1]
    acts[:8] = jnp.zeros((8, 48, 256), BF16)
    acts[56:] = jnp.zeros((8, 48, 256), BF16)
    for pieces, side in ((own, core), (other, 1 - core)):
        for d in range(16):
            j = torus_at(y, x, d, -1)
            half = j // 8
            strip = 2 * (j % 8) + side
            lanes = pl.ds(pl.multiple_of(half * 128, 128), 128)
            acts[pl.ds(3 * strip + 8, 3), :, lanes] = pieces[d][:144, :].reshape(3, 48, 128)
            wide[:, strip, :, lanes] = pieces[d][144:, :].reshape(18, 16, 128)

    top = 24 * core - 8
    left = 160 * z + 10 * (4 * y + x) - 8

    def inside(start, rows):
        r = lax.broadcasted_iota(jnp.int32, (rows, W, 256), 0) + (top + start)
        c = lax.broadcasted_iota(jnp.int32, (rows, W, 256), 1) + left
        return (r >= 0) & (r < 48) & (c >= 0) & (c < 1280)

    def tap(which, i, j):
        return wide[9 * which + 3 * i + j].reshape(256, 256)

    def ahead(source, start, rows, which):
        band = jnp.concatenate(
            [source[pl.ds(start + 2 * i - 2, rows), :W, :] for i in range(3)], axis=-1
        ).reshape(rows * W, 768)
        total = None
        for j in range(3):
            weights = jnp.concatenate([tap(which, i, j) for i in range(3)], axis=0)
            term = jnp.dot(band, weights, preferred_element_type=F32)
            if j != 1:
                term = pltpu.roll(term, (rows * W - 2 * (j - 1)) % (rows * W), 0)
            total = term if total is None else total + term
        return total.reshape(rows, W, 256)

    def backward(source, start, rows, which):
        band = jnp.concatenate(
            [source[pl.ds(start - 2 * i + 2, rows), :, :] for i in range(3)], axis=-1
        ).reshape(rows * W, 768)
        total = None
        for j in range(3):
            weights = jnp.concatenate([tap(which, i, j) for i in range(3)], axis=1)
            term = lax.dot_general(
                band, weights, (((1,), (1,)), ((), ())), preferred_element_type=F32
            )
            if j != 1:
                term = pltpu.roll(term, (rows * W + 2 * (j - 1)) % (rows * W), 0)
            total = term if total is None else total + term
        return total.reshape(rows, W, 256)

    def slope(v):
        s = sigmoid(v)
        return s * (1.0 + v * (1.0 - s))

    def each(start, count, rows, body):
        def step(k, _):
            body(start + k * rows)
            return 0

        lax.fori_loop(0, count, step, 0)

    def first_step(start):
        rows = 12
        value = ahead(acts, start + 24 * core, rows, 0)
        pre[pl.ds(start, rows)] = value
        value = jnp.where(inside(start, rows), value * sigmoid(value), 0.0)
        hidden[pl.ds(start, rows)] = value.astype(BF16)

    each(2, 3, 12, first_step)

    def second_step(start):
        rows = 16
        value = ahead(hidden, start, rows, 1)
        got = acts[pl.ds(start + 24 * core, rows), 16:, :].astype(F32).reshape(rows * W, 256)
        got = pltpu.roll(got, rows * W - 6, 0).reshape(rows, W, 256)
        value = jnp.where(inside(start, rows), got * slope(value), 0.0)
        second[pl.ds(start, rows)] = value.astype(BF16)

    each(4, 2, 16, second_step)

    def third_step(start):
        rows = 14
        value = backward(second, start, rows, 1)
        value = jnp.where(inside(start, rows), value * slope(pre[pl.ds(start, rows)]), 0.0)
        first[pl.ds(start, rows)] = value.astype(BF16)

    each(6, 2, 14, third_step)

    def fourth_step(start):
        rows = 12
        value = backward(first, start, rows, 0)
        image_rows[pl.ds(start - 8, rows)] = value[:, 8:24, :].astype(BF16)

    each(8, 2, 12, fourth_step)
    for side, out in ((1 - core, image_send), (core, image_keep)):
        for k in range(4):
            for half in range(2):
                out[half, k] = image_rows[
                    pl.ds(6 * k + 3 * side, 3), :, 128 * half : 128 * half + 128
                ].reshape(48, 128)

    def weight_terms(values, grads, which):
        turned = values.reshape(28 * W, 256).astype(F32).T.astype(BF16)
        column = lax.broadcasted_iota(jnp.int32, (24, W, 256), 1)
        chosen = jnp.where((column >= 8) & (column < 18), grads[8:32].astype(F32), 0.0)
        chosen = chosen.reshape(24 * W, 256)
        for j in range(3):
            shifted = chosen
            if j != 1:
                shifted = pltpu.roll(chosen, (24 * W + 2 * (j - 1)) % (24 * W), 0)
            mine[j, 8:32] = shifted.reshape(24, W, 256).astype(BF16)
        for i in range(3):
            for j in range(3):
                rows = mine[j, 8 - 2 * i : 36 - 2 * i].reshape(28 * W, 256)
                got = jnp.dot(turned, rows, preferred_element_type=F32).astype(BF16)
                got = got.reshape(8, 2, 16, 256)
                for side in range(2):
                    for half in range(2):
                        terms[side, half, :, 9 * which + 3 * i + j] = got[
                            :, side, :, 128 * half : 128 * half + 128
                        ]

    for j in range(3):
        mine[j, :8] = jnp.zeros((8, W, 256), BF16)
        mine[j, 32:] = jnp.zeros((8, W, 256), BF16)
    weight_terms(hidden[6:34], second, 1)
    weight_terms(acts[pl.ds(6 + 24 * core, 28), :W, :], first, 0)
    send[...] = terms[1 - core].reshape(2, 8, 288, 128)
    keep[...] = terms[core].reshape(2, 8, 288, 128)


def scatter_kernel(at, keep, got, image_keep, image_got, *outs):
    for d in range(16):
        j = torus_at(at[2], at[3], d, 1)
        half, q = j // 8, j % 8
        outs[d][:288, :] = (keep[half, q].astype(F32) + got[half, q].astype(F32)).astype(BF16)
        mine = (q // 4) == at[4]
        outs[d][288:, :] = jnp.where(
            mine, image_keep[half, q % 4].astype(F32), image_got[half, q % 4].astype(F32)
        ).astype(BF16)


def regroup_kernel(at, *rest):
    pieces, outs, (held, columns, windows) = rest[:16], rest[16:24], rest[24:]
    total = None
    for d in range(16):
        held[torus_at(at[2], at[3], d, -1)] = pieces[d][288:, :]
        term = pieces[d][:288, :].astype(F32)
        total = term if total is None else total + term
    total = jnp.concatenate([total, jnp.zeros((96, 128), F32)], axis=0).T.astype(BF16)
    for z in range(8):
        windows[z, 48:, :] = total[16 * z : 16 * z + 16]
        windows[z, :48, 256:] = jnp.zeros((48, 128), BF16)
    columns[...] = jnp.zeros((256, 128), F32)
    for i in range(3):
        for j in range(16):
            columns[10 * j : 10 * j + 16, :] = held[j, 16 * i : 16 * i + 16, :].astype(F32)
        turned = columns[...].T.astype(BF16)
        for z in range(8):
            windows[z, 16 * i : 16 * i + 16, :256] = turned[16 * z : 16 * z + 16]
    for d in range(8):
        outs[d][...] = windows[(at[1] + d) % 8]


def finish_kernel(scale, at, *rest):
    pieces, (image_out, filters_out), (held, wide) = rest[:8], rest[8:10], rest[10:]
    total = None
    for d in range(8):
        held[(at[1] - d + 8) % 8] = pieces[d][...]
        term = pieces[d][48:, :].astype(F32)
        total = term if total is None else total + term
    filters_out[...] = total * scale
    lane = lax.broadcasted_iota(jnp.int32, (48, 384), 1)
    wide[...] = jnp.zeros((48, 1536), F32)
    for z in range(8):
        base = 160 * z // 128 * 128
        off = 160 * z - base
        value = held[z, :48, :].astype(F32)
        if off:
            value = pltpu.roll(value, off, 1)
        wide[:, base : base + 384] = jnp.where(
            (lane >= off) & (lane < off + 160), value, wide[:, base : base + 384]
        )
    image_out[...] = wide[:, :1280].astype(BF16)


def along_z(pieces):
    return [pieces[0]] + [
        lax.ppermute(pieces[d], "z", [(k, (k + d) % 8) for k in range(8)]) for d in range(1, 8)
    ]


def along_torus(pieces):
    def to(k, d):
        return (k // 4 + d // 4) % 4 * 4 + (k + d) % 4

    return [pieces[0]] + [
        lax.ppermute(pieces[d], TORUS, [(k, to(k, d)) for k in range(16)]) for d in range(1, 16)
    ]


def swapped(array):
    return lax.ppermute(array, "core", [(0, 1), (1, 0)])


def local(image, filter_one, filter_two, cotangent):
    scale = 1.0 / math.sqrt(48 * 1280)
    yh, z, yl, x, core = (lax.axis_index(a) for a in AXES)
    at = jnp.stack([yh, z, 2 * yh + yl, x, core]).astype(jnp.int32)

    def rows_first(a):
        return jnp.transpose(a, (1, 0, 2)).reshape(48, 1280)

    filters = jnp.concatenate(
        [jnp.transpose(f, (2, 1, 0)).reshape(16, 144) for f in (filter_one, filter_two)]
        + [jnp.zeros((16, 96), BF16)],
        axis=1,
    )
    pieces = call(
        windows_kernel,
        [shape((64, 384))] * 8,
        [pltpu.VMEM((48, 1792), F32), pltpu.VMEM((48, 1792), F32), pltpu.VMEM((8, 64, 384), BF16)],
        [rows_first(image), rows_first(cotangent), filters],
        at,
    )
    pieces = along_z(pieces)
    pieces = call(
        turn_kernel,
        [shape((432, 128))] * 16,
        [
            pltpu.VMEM((8, 64, 384), BF16),
            pltpu.VMEM((384, 128), F32),
            pltpu.VMEM((48, 128), F32),
            pltpu.VMEM((16, 144, 128), BF16),
        ],
        pieces,
        at,
    )
    pieces = along_torus(pieces)
    others = [swapped(p) for p in pieces]
    send, keep, image_send, image_keep = call(
        conv_kernel,
        [shape((2, 8, 288, 128))] * 2 + [shape((2, 4, 48, 128))] * 2,
        [
            pltpu.VMEM((64, 48, 256), BF16),
            pltpu.VMEM((18, 16, 16, 256), BF16),
            pltpu.VMEM((40, W, 256), F32),
            pltpu.VMEM((40, W, 256), BF16),
            pltpu.VMEM((40, W, 256), BF16),
            pltpu.VMEM((40, W, 256), BF16),
            pltpu.VMEM((3, 40, W, 256), BF16),
            pltpu.VMEM((2, 2, 8, 18, 16, 128), BF16),
            pltpu.VMEM((24, 16, 256), BF16),
        ],
        [*pieces, *others],
        at,
    )
    pieces = call(
        scatter_kernel,
        [shape((336, 128))] * 16,
        [],
        [keep, swapped(send), image_keep, swapped(image_send)],
        at,
    )
    pieces = along_torus(pieces)
    pieces = call(
        regroup_kernel,
        [shape((64, 384))] * 8,
        [
            pltpu.VMEM((16, 48, 128), BF16),
            pltpu.VMEM((256, 128), F32),
            pltpu.VMEM((8, 64, 384), BF16),
        ],
        pieces,
        at,
    )
    pieces = along_z(pieces)
    image_grad, filter_grads = call(
        functools.partial(finish_kernel, scale),
        [shape((48, 1280)), shape((16, 384), F32)],
        [pltpu.VMEM((8, 64, 384), BF16), pltpu.VMEM((48, 1536), F32)],
        pieces,
        at,
    )
    grad_one, grad_two = (
        jnp.transpose(filter_grads[:, 144 * k : 144 * k + 144].reshape(16, 9, 16), (2, 1, 0))
        for k in range(2)
    )
    return jnp.transpose(image_grad.reshape(3, 16, 1280), (1, 0, 2)), grad_one, grad_two


def solution(mesh):
    finer = Mesh(mesh.devices.reshape(2, 8, 2, 4, 2), AXES)
    return jax.shard_map(
        local,
        mesh=finer,
        in_specs=(
            P(CHAN, STRIP, None),
            P(STRIP, None, CHAN),
            P(STRIP, None, CHAN),
            P(CHAN, STRIP, None),
        ),
        out_specs=(P(CHAN, STRIP, None), P(STRIP, None, CHAN), P(STRIP, None, CHAN)),
        check_vma=False,
    )
```

```python
import functools
import math

import jax
import jax.numpy as jnp
from jax import lax
from jax.experimental import pallas as pl
from jax.experimental.pallas import tpu as pltpu
from jax.sharding import Mesh
from jax.sharding import PartitionSpec as P

AXES = ("yh", "z", "yl", "x", "core")
CHAN = ("yh", "z")
STRIP = ("yl", "x", "core")
TORUS = ("yh", "yl", "x")
F32 = jnp.float32
BF16 = jnp.bfloat16

W = 32


def call(kernel, outs, scratch, args, prefetch, room=10):
    return pl.pallas_call(
        kernel,
        out_shape=outs,
        in_specs=[pl.BlockSpec(memory_space=pltpu.SMEM)]
        + [pl.BlockSpec(memory_space=pltpu.VMEM)] * len(args),
        out_specs=jax.tree.map(lambda _: pl.BlockSpec(memory_space=pltpu.VMEM), outs),
        scratch_shapes=scratch,
        compiler_params=pltpu.CompilerParams(vmem_limit_bytes=room * 2**20),
    )(prefetch, *args)


def shape(dims, kind=BF16):
    return jax.ShapeDtypeStruct(dims, kind)


def windows_kernel(at, image, cotangent, pieces, *rest):
    windows, image_wide, cotangent_wide = rest
    for wide, source in ((image_wide, image), (cotangent_wide, cotangent)):
        wide[:, :256] = jnp.zeros((48, 256), F32)
        wide[:, 1536:] = jnp.zeros((48, 256), F32)
        wide[:, 256:1536] = source[...].astype(F32)
    lane = lax.broadcasted_iota(jnp.int32, (48, 384), 1)
    for z in range(8):
        first = 256 + 160 * z - 8
        base = first // 128 * 128
        left = pltpu.roll(image_wide[:, base : base + 384], 384 - (first - base), 1)
        second = 256 + 160 * z - 4 - 176
        base = second // 128 * 128
        right = pltpu.roll(cotangent_wide[:, base : base + 512], 512 - (second - base), 1)[:, :384]
        windows[z, :48, :] = jnp.where(lane < 176, left, right).astype(BF16)
        windows[z, 48:, :] = pieces[...]


def turn_kernel(at, *rest):
    held, outs, turned, chunk = rest
    for i in range(3):
        turned[...] = held[:, 16 * i : 16 * i + 16, :].reshape(128, 384).astype(F32).T
        for j in range(16):
            chunk[:32, :] = turned[10 * j : 10 * j + 32, :]
            chunk[26:48, :] = turned[176 + 10 * j : 198 + 10 * j, :]
            outs[j, 48 * i : 48 * i + 48, :] = chunk[...].astype(BF16)
    filters = held[:, 48:, :].reshape(128, 384).astype(F32).T[:288].astype(BF16)
    for j in range(16):
        outs[j, 144:, :] = filters


def sigmoid(v):
    return 1.0 / (1.0 + jnp.exp(-v))


def conv_kernel(at, *rest):
    own, other = rest[:2]
    send, keep, image_send, image_keep = rest[2:6]
    acts, wide, pre, hidden, second, first, mine, terms, image_rows = rest[6:]
    y, x, core, z = at[2], at[3], at[4], at[1]
    acts[:8] = jnp.zeros((8, 48, 256), BF16)
    acts[56:] = jnp.zeros((8, 48, 256), BF16)
    for pieces, side in ((own, core), (other, 1 - core)):
        for j in range(16):
            half = j // 8
            strip = 2 * (j % 8) + side
            lanes = slice(half * 128, half * 128 + 128)
            acts[pl.ds(3 * strip + 8, 3), :, lanes] = pieces[j, :144, :].reshape(3, 48, 128)
            wide[:, strip, :, lanes] = pieces[j, 144:, :].reshape(18, 16, 128)

    top = 24 * core - 8
    left = 160 * z + 10 * (4 * y + x) - 8

    def inside(start, rows):
        r = lax.broadcasted_iota(jnp.int32, (rows, W, 256), 0) + (top + start)
        c = lax.broadcasted_iota(jnp.int32, (rows, W, 256), 1) + left
        return (r >= 0) & (r < 48) & (c >= 0) & (c < 1280)

    def tap(which, i, j):
        return wide[9 * which + 3 * i + j].reshape(256, 256)

    def ahead(source, start, rows, which):
        band = jnp.concatenate(
            [source[pl.ds(start + 2 * i - 2, rows), :W, :] for i in range(3)], axis=-1
        ).reshape(rows * W, 768)
        total = None
        for j in range(3):
            weights = jnp.concatenate([tap(which, i, j) for i in range(3)], axis=0)
            term = jnp.dot(band, weights, preferred_element_type=F32)
            if j != 1:
                term = pltpu.roll(term, (rows * W - 2 * (j - 1)) % (rows * W), 0)
            total = term if total is None else total + term
        return total.reshape(rows, W, 256)

    def backward(source, start, rows, which):
        band = jnp.concatenate(
            [source[pl.ds(start - 2 * i + 2, rows), :, :] for i in range(3)], axis=-1
        ).reshape(rows * W, 768)
        total = None
        for j in range(3):
            weights = jnp.concatenate([tap(which, i, j) for i in range(3)], axis=1)
            term = lax.dot_general(
                band, weights, (((1,), (1,)), ((), ())), preferred_element_type=F32
            )
            if j != 1:
                term = pltpu.roll(term, (rows * W + 2 * (j - 1)) % (rows * W), 0)
            total = term if total is None else total + term
        return total.reshape(rows, W, 256)

    def slope(v):
        s = sigmoid(v)
        return s * (1.0 + v * (1.0 - s))

    def each(start, count, rows, body):
        def step(k, _):
            body(start + k * rows)
            return 0

        lax.fori_loop(0, count, step, 0)

    def first_step(start):
        rows = 12
        value = ahead(acts, start + 24 * core, rows, 0)
        pre[pl.ds(start, rows)] = value
        value = jnp.where(inside(start, rows), value * sigmoid(value), 0.0)
        hidden[pl.ds(start, rows)] = value.astype(BF16)

    each(2, 3, 12, first_step)

    def second_step(start):
        rows = 16
        value = ahead(hidden, start, rows, 1)
        got = acts[pl.ds(start + 24 * core, rows), 16:, :].astype(F32).reshape(rows * W, 256)
        got = pltpu.roll(got, rows * W - 6, 0).reshape(rows, W, 256)
        value = jnp.where(inside(start, rows), got * slope(value), 0.0)
        second[pl.ds(start, rows)] = value.astype(BF16)

    each(4, 2, 16, second_step)

    def third_step(start):
        rows = 14
        value = backward(second, start, rows, 1)
        value = jnp.where(inside(start, rows), value * slope(pre[pl.ds(start, rows)]), 0.0)
        first[pl.ds(start, rows)] = value.astype(BF16)

    each(6, 2, 14, third_step)

    def fourth_step(start):
        rows = 12
        value = backward(first, start, rows, 0)
        image_rows[pl.ds(start - 8, rows)] = value[:, 8:24, :].astype(BF16)

    each(8, 2, 12, fourth_step)
    for side, out in ((1 - core, image_send), (core, image_keep)):
        for k in range(4):
            for half in range(2):
                out[half, k] = image_rows[
                    pl.ds(6 * k + 3 * side, 3), :, 128 * half : 128 * half + 128
                ].reshape(48, 128)

    def weight_terms(values, grads, which):
        turned = values.reshape(28 * W, 256).astype(F32).T.astype(BF16)
        column = lax.broadcasted_iota(jnp.int32, (24, W, 256), 1)
        chosen = jnp.where((column >= 8) & (column < 18), grads[8:32].astype(F32), 0.0)
        chosen = chosen.reshape(24 * W, 256)
        for j in range(3):
            shifted = chosen
            if j != 1:
                shifted = pltpu.roll(chosen, (24 * W + 2 * (j - 1)) % (24 * W), 0)
            mine[j, 8:32] = shifted.reshape(24, W, 256).astype(BF16)
        def step(i, _):
            for j in range(3):
                rows = mine[j, pl.ds(8 - 2 * i, 28)].reshape(28 * W, 256)
                got = jnp.dot(turned, rows, preferred_element_type=F32).astype(BF16)
                got = got.reshape(8, 2, 16, 256)
                for side in range(2):
                    for half in range(2):
                        terms[side, half, :, 9 * which + 3 * i + j] = got[
                            :, side, :, 128 * half : 128 * half + 128
                        ]
            return 0

        lax.fori_loop(0, 3, step, 0)

    for j in range(3):
        mine[j, :8] = jnp.zeros((8, W, 256), BF16)
        mine[j, 32:] = jnp.zeros((8, W, 256), BF16)
    weight_terms(hidden[6:34], second, 1)
    weight_terms(acts[pl.ds(6 + 24 * core, 28), :W, :], first, 0)
    send[...] = terms[1 - core].reshape(2, 8, 288, 128)
    keep[...] = terms[core].reshape(2, 8, 288, 128)


def scatter_kernel(at, keep, got, image_keep, image_got, outs):
    for j in range(16):
        half, q = j // 8, j % 8
        outs[j, :288, :] = (keep[half, q].astype(F32) + got[half, q].astype(F32)).astype(BF16)
    for half in range(2):
        for k in range(4):
            outs[8 * half + 4 * at[4] + k, 288:, :] = image_keep[half, k]
            outs[8 * half + 4 - 4 * at[4] + k, 288:, :] = image_got[half, k]


def regroup_kernel(at, *rest):
    pieces, windows, columns = rest
    total = None
    for j in range(16):
        term = pieces[j, :288, :].astype(F32)
        total = term if total is None else total + term
    total = jnp.concatenate([total, jnp.zeros((96, 128), F32)], axis=0).T.astype(BF16)
    for z in range(8):
        windows[z, 48:, :] = total[16 * z : 16 * z + 16]
        windows[z, :48, 256:] = jnp.zeros((48, 128), BF16)
    columns[...] = jnp.zeros((256, 128), F32)
    for i in range(3):
        for j in range(16):
            columns[10 * j : 10 * j + 16, :] = pieces[j, 288 + 16 * i : 304 + 16 * i, :].astype(
                F32
            )
        turned = columns[...].T.astype(BF16)
        for z in range(8):
            windows[z, 16 * i : 16 * i + 16, :256] = turned[16 * z : 16 * z + 16]


def finish_kernel(scale, at, *rest):
    pieces, image_out, filters_out, wide = rest
    total = None
    for z in range(8):
        term = pieces[z, 48:, :].astype(F32)
        total = term if total is None else total + term
    filters_out[...] = total * scale
    lane = lax.broadcasted_iota(jnp.int32, (48, 384), 1)
    wide[...] = jnp.zeros((48, 1536), F32)
    for z in range(8):
        base = 160 * z // 128 * 128
        off = 160 * z - base
        value = pieces[z, :48, :].astype(F32)
        if off:
            value = pltpu.roll(value, off, 1)
        wide[:, base : base + 384] = jnp.where(
            (lane >= off) & (lane < off + 160), value, wide[:, base : base + 384]
        )
    image_out[...] = wide[:, :1280].astype(BF16)


def exchanged(array, axes):
    return lax.all_to_all(array, axes, split_axis=0, concat_axis=0, tiled=True)


def swapped(array):
    return lax.ppermute(array, "core", [(0, 1), (1, 0)])


def local(image, filter_one, filter_two, cotangent):
    scale = 1.0 / math.sqrt(48 * 1280)
    yh, z, yl, x, core = (lax.axis_index(a) for a in AXES)
    at = jnp.stack([yh, z, 2 * yh + yl, x, core]).astype(jnp.int32)

    def rows_first(a):
        return jnp.transpose(a, (1, 0, 2)).reshape(48, 1280)

    filters = jnp.concatenate(
        [jnp.transpose(f, (2, 1, 0)).reshape(16, 144) for f in (filter_one, filter_two)]
        + [jnp.zeros((16, 96), BF16)],
        axis=1,
    )
    pieces = call(
        windows_kernel,
        shape((8, 64, 384)),
        [pltpu.VMEM((48, 1792), F32), pltpu.VMEM((48, 1792), F32)],
        [rows_first(image), rows_first(cotangent), filters],
        at,
    )
    pieces = call(
        turn_kernel,
        shape((16, 432, 128)),
        [pltpu.VMEM((384, 128), F32), pltpu.VMEM((48, 128), F32)],
        [exchanged(pieces, "z")],
        at,
    )
    pieces = exchanged(pieces, TORUS)
    send, keep, image_send, image_keep = call(
        conv_kernel,
        [shape((2, 8, 288, 128))] * 2 + [shape((2, 4, 48, 128))] * 2,
        [
            pltpu.VMEM((64, 48, 256), BF16),
            pltpu.VMEM((18, 16, 16, 256), BF16),
            pltpu.VMEM((40, W, 256), F32),
            pltpu.VMEM((40, W, 256), BF16),
            pltpu.VMEM((40, W, 256), BF16),
            pltpu.VMEM((40, W, 256), BF16),
            pltpu.VMEM((3, 40, W, 256), BF16),
            pltpu.VMEM((2, 2, 8, 18, 16, 128), BF16),
            pltpu.VMEM((24, 16, 256), BF16),
        ],
        [pieces, swapped(pieces)],
        at,
        28,
    )
    pieces = call(
        scatter_kernel,
        shape((16, 336, 128)),
        [],
        [keep, swapped(send), image_keep, swapped(image_send)],
        at,
    )
    pieces = call(
        regroup_kernel,
        shape((8, 64, 384)),
        [pltpu.VMEM((256, 128), F32)],
        [exchanged(pieces, TORUS)],
        at,
    )
    image_grad, filter_grads = call(
        functools.partial(finish_kernel, scale),
        [shape((48, 1280)), shape((16, 384), F32)],
        [pltpu.VMEM((48, 1536), F32)],
        [exchanged(pieces, "z")],
        at,
    )
    grad_one, grad_two = (
        jnp.transpose(filter_grads[:, 144 * k : 144 * k + 144].reshape(16, 9, 16), (2, 1, 0))
        for k in range(2)
    )
    return jnp.transpose(image_grad.reshape(3, 16, 1280), (1, 0, 2)), grad_one, grad_two


def solution(mesh):
    finer = Mesh(mesh.devices.reshape(2, 8, 2, 4, 2), AXES)
    return jax.shard_map(
        local,
        mesh=finer,
        in_specs=(
            P(CHAN, STRIP, None),
            P(STRIP, None, CHAN),
            P(STRIP, None, CHAN),
            P(CHAN, STRIP, None),
        ),
        out_specs=(P(CHAN, STRIP, None), P(STRIP, None, CHAN), P(STRIP, None, CHAN)),
        check_vma=False,
    )
```

```python
import functools
import math

import jax
import jax.numpy as jnp
from jax import lax
from jax.experimental import pallas as pl
from jax.experimental.pallas import tpu as pltpu
from jax.sharding import Mesh
from jax.sharding import PartitionSpec as P

AXES = ("yh", "z", "yl", "x", "core")
CHAN = ("yh", "z")
STRIP = ("yl", "x", "core")
TORUS = ("yh", "yl", "x")
F32 = jnp.float32
BF16 = jnp.bfloat16

W = 32


def call(kernel, outs, scratch, args, prefetch, room=10, space=pltpu.VMEM):
    return pl.pallas_call(
        kernel,
        out_shape=outs,
        in_specs=[pl.BlockSpec(memory_space=pltpu.SMEM)]
        + [pl.BlockSpec(memory_space=space)] * len(args),
        out_specs=jax.tree.map(lambda _: pl.BlockSpec(memory_space=pltpu.VMEM), outs),
        scratch_shapes=scratch,
        compiler_params=pltpu.CompilerParams(vmem_limit_bytes=room * 2**20),
    )(prefetch, *args)


def shape(dims, kind=BF16):
    return jax.ShapeDtypeStruct(dims, kind)


def windows_kernel(at, *rest):
    sources, (windows, image_wide, cotangent_wide), held, arrived = (
        rest[:4],
        rest[4:7],
        rest[7:11],
        rest[11],
    )
    copies = [
        pltpu.make_async_copy(a, b, arrived.at[k]) for k, (a, b) in enumerate(zip(sources, held))
    ]
    for copy in copies:
        copy.start()
    for copy in copies:
        copy.wait()
    image, cotangent, filter_one, filter_two = held
    row = lax.broadcasted_iota(jnp.int32, (16, 16), 0)
    unit = (row == lax.broadcasted_iota(jnp.int32, (16, 16), 1)).astype(F32).astype(BF16)
    pieces = jnp.concatenate(
        [
            lax.dot_general(
                unit, f[...], (((1,), (1,)), ((), ())), preferred_element_type=F32
            )
            for f in (filter_one, filter_two)
        ]
        + [jnp.zeros((16, 96), F32)],
        axis=1,
    ).astype(BF16)
    for wide, source in ((image_wide, image), (cotangent_wide, cotangent)):
        wide[:, :256] = jnp.zeros((48, 256), F32)
        wide[:, 1536:] = jnp.zeros((48, 256), F32)
        wide[:, 256:1536] = source[...].astype(F32)
    lane = lax.broadcasted_iota(jnp.int32, (48, 384), 1)
    for z in range(8):
        first = 256 + 160 * z - 8
        base = first // 128 * 128
        left = pltpu.roll(image_wide[:, base : base + 384], 384 - (first - base), 1)
        second = 256 + 160 * z - 4 - 176
        base = second // 128 * 128
        right = pltpu.roll(cotangent_wide[:, base : base + 512], 512 - (second - base), 1)[:, :384]
        windows[z, :48, :] = jnp.where(lane < 176, left, right).astype(BF16)
        windows[z, 48:, :] = pieces


def turn_kernel(at, *rest):
    held, outs, turned, chunk = rest
    for i in range(3):
        turned[...] = held[:, 16 * i : 16 * i + 16, :].reshape(128, 384).astype(F32).T
        for j in range(16):
            chunk[:32, :] = turned[10 * j : 10 * j + 32, :]
            chunk[26:48, :] = turned[176 + 10 * j : 198 + 10 * j, :]
            outs[j, 48 * i : 48 * i + 48, :] = chunk[...].astype(BF16)
    filters = held[:, 48:, :].reshape(128, 384).astype(F32).T[:288].astype(BF16)
    for j in range(16):
        outs[j, 144:, :] = filters


def sigmoid(v):
    return 0.5 + 0.5 * jnp.tanh(0.5 * v)


def conv_kernel(at, *rest):
    own, other = rest[:2]
    send, keep, image_send, image_keep = rest[2:6]
    acts, wide, pre, hidden, second, first, mine, terms, image_rows = rest[6:]
    y, x, core, z = at[2], at[3], at[4], at[1]
    acts[:8] = jnp.zeros((8, 48, 256), BF16)
    acts[56:] = jnp.zeros((8, 48, 256), BF16)
    for pieces, side in ((own, core), (other, 1 - core)):
        for j in range(16):
            half = j // 8
            strip = 2 * (j % 8) + side
            lanes = slice(half * 128, half * 128 + 128)
            acts[pl.ds(3 * strip + 8, 3), :, lanes] = pieces[j, :144, :].reshape(3, 48, 128)
            wide[:, strip, :, lanes] = pieces[j, 144:, :].reshape(18, 16, 128)

    at_left = (z == 0) & (y + x == 0)
    at_right = (z == 7) & (y + x == 6)

    def cleared(target):
        @pl.when(core == 0)
        def _():
            target[:8] = jnp.zeros((8, W, 256), BF16)

        @pl.when(core == 1)
        def _():
            target[32:] = jnp.zeros((8, W, 256), BF16)

        @pl.when(at_left)
        def _():
            target[:, :8, :] = jnp.zeros((40, 8, 256), BF16)

        @pl.when(at_right)
        def _():
            target[:, 18:, :] = jnp.zeros((40, 14, 256), BF16)

    def tap(which, i, j):
        return wide[9 * which + 3 * i + j].reshape(256, 256)

    def ahead(source, start, rows, which):
        band = jnp.concatenate(
            [source[pl.ds(start + 2 * i - 2, rows), :W, :] for i in range(3)], axis=-1
        ).reshape(rows * W, 768)
        total = None
        for j in range(3):
            weights = jnp.concatenate([tap(which, i, j) for i in range(3)], axis=0)
            term = jnp.dot(band, weights, preferred_element_type=F32)
            if j != 1:
                term = pltpu.roll(term, (rows * W - 2 * (j - 1)) % (rows * W), 0)
            total = term if total is None else total + term
        return total.reshape(rows, W, 256)

    def backward(source, start, rows, which):
        band = jnp.concatenate(
            [source[pl.ds(start - 2 * i + 2, rows), :, :] for i in range(3)], axis=-1
        ).reshape(rows * W, 768)
        total = None
        for j in range(3):
            weights = jnp.concatenate([tap(which, i, j) for i in range(3)], axis=1)
            term = lax.dot_general(
                band, weights, (((1,), (1,)), ((), ())), preferred_element_type=F32
            )
            if j != 1:
                term = pltpu.roll(term, (rows * W + 2 * (j - 1)) % (rows * W), 0)
            total = term if total is None else total + term
        return total.reshape(rows, W, 256)

    def slope(v):
        s = sigmoid(v)
        return s * (1.0 + v * (1.0 - s))

    def each(start, count, rows, body):
        def step(k, _):
            body(start + k * rows)
            return 0

        lax.fori_loop(0, count, step, 0)

    def first_step(start):
        rows = 12
        value = ahead(acts, start + 24 * core, rows, 0)
        pre[pl.ds(start, rows)] = value
        hidden[pl.ds(start, rows)] = (value * sigmoid(value)).astype(BF16)

    each(2, 3, 12, first_step)
    cleared(hidden)

    def second_step(start):
        rows = 16
        value = ahead(hidden, start, rows, 1)
        got = acts[pl.ds(start + 24 * core, rows), 16:, :].astype(F32).reshape(rows * W, 256)
        got = pltpu.roll(got, rows * W - 6, 0).reshape(rows, W, 256)
        second[pl.ds(start, rows)] = (got * slope(value)).astype(BF16)

    each(4, 2, 16, second_step)
    cleared(second)

    def third_step(start):
        rows = 14
        value = backward(second, start, rows, 1)
        first[pl.ds(start, rows)] = (value * slope(pre[pl.ds(start, rows)])).astype(BF16)

    each(6, 2, 14, third_step)
    cleared(first)

    def fourth_step(start):
        rows = 12
        value = backward(first, start, rows, 0)
        image_rows[pl.ds(start - 8, rows)] = value[:, 8:24, :].astype(BF16)

    each(8, 2, 12, fourth_step)
    for side, out in ((1 - core, image_send), (core, image_keep)):
        for k in range(4):
            for half in range(2):
                out[half, k] = image_rows[
                    pl.ds(6 * k + 3 * side, 3), :, 128 * half : 128 * half + 128
                ].reshape(48, 128)

    def narrowed(values, rows, shift):
        flat = values.astype(F32).reshape(rows * W, 256)
        flat = pltpu.roll(flat, (rows * W + shift) % (rows * W), 0)
        return flat.reshape(rows, W, 256)[:, :16, :]

    def weight_terms(values, grads, which):
        turned = narrowed(values, 28, -6).reshape(28 * 16, 256).T.astype(BF16)
        column = lax.broadcasted_iota(jnp.int32, (24, 16, 256), 1)
        for j in range(3):
            kept = (column >= 2 * j) & (column < 2 * j + 10)
            shifted = narrowed(grads[8:32], 24, 2 * j - 8)
            mine[j, 8:32] = jnp.where(kept, shifted, 0.0).astype(BF16)

        def step(i, _):
            for j in range(3):
                rows = mine[j, pl.ds(8 - 2 * i, 28)].reshape(28 * 16, 256)
                got = jnp.dot(turned, rows, preferred_element_type=F32).astype(BF16)
                got = got.reshape(8, 2, 16, 256)
                for side in range(2):
                    for half in range(2):
                        terms[side, half, :, 9 * which + 3 * i + j] = got[
                            :, side, :, 128 * half : 128 * half + 128
                        ]
            return 0

        lax.fori_loop(0, 3, step, 0)

    for j in range(3):
        mine[j, :8] = jnp.zeros((8, 16, 256), BF16)
        mine[j, 32:] = jnp.zeros((8, 16, 256), BF16)
    weight_terms(hidden[6:34], second, 1)
    weight_terms(acts[pl.ds(6 + 24 * core, 28), :W, :], first, 0)
    send[...] = terms[1 - core].reshape(2, 8, 288, 128)
    keep[...] = terms[core].reshape(2, 8, 288, 128)


def scatter_kernel(at, keep, got, image_keep, image_got, outs):
    for j in range(16):
        half, q = j // 8, j % 8
        outs[j, :288, :] = (keep[half, q].astype(F32) + got[half, q].astype(F32)).astype(BF16)
    for half in range(2):
        for k in range(4):
            outs[8 * half + 4 * at[4] + k, 288:, :] = image_keep[half, k]
            outs[8 * half + 4 - 4 * at[4] + k, 288:, :] = image_got[half, k]


def regroup_kernel(at, *rest):
    pieces, windows, columns = rest
    total = None
    for j in range(16):
        term = pieces[j, :288, :].astype(F32)
        total = term if total is None else total + term
    total = jnp.concatenate([total, jnp.zeros((96, 128), F32)], axis=0).T
    for z in range(8):
        windows[z, 48:64, :] = total[16 * z : 16 * z + 16, :128].astype(BF16)
        windows[z, 64:80, :] = total[16 * z : 16 * z + 16, 128:256].astype(BF16)
    lane = lax.broadcasted_iota(jnp.int32, (128, 128), 1)
    rest = pltpu.roll(total[:, 256:], 96, 1)
    columns[...] = jnp.zeros((256, 128), F32)
    for i in range(3):
        for j in range(16):
            columns[10 * j : 10 * j + 16, :] = pieces[j, 288 + 16 * i : 304 + 16 * i, :].astype(
                F32
            )
        turned = columns[...].T
        for z in range(8):
            windows[z, 16 * i : 16 * i + 16, :] = turned[16 * z : 16 * z + 16, :128].astype(BF16)
        end = turned[:, 128:]
        if i:
            end = pltpu.roll(end, 32 * i, 1)
        rest = jnp.where((lane >= 32 * i) & (lane < 32 * i + 32), end, rest)
    for z in range(8):
        windows[z, 80:, :] = rest[16 * z : 16 * z + 16].astype(BF16)


def finish_kernel(scale, at, pieces, image_out, grad_one, grad_two, wide):
    total = None
    for z in range(8):
        parts = [pieces[z, k : k + 16, :].astype(F32) for k in (48, 64, 80)]
        total = parts if total is None else [t + p for t, p in zip(total, parts)]
    total[2] = pltpu.roll(total[2], 32, 1)
    total = jnp.concatenate(total, axis=1) * scale
    for out, at_lane in ((grad_one, 0), (grad_two, 144)):
        part = total if at_lane == 0 else pltpu.roll(total, 384 - at_lane, 1)
        out[...] = jnp.concatenate([part[:, :256], jnp.zeros((112, 256), F32)], axis=0).T[:144, :16]
    lane = lax.broadcasted_iota(jnp.int32, (48, 384), 1)
    wide[...] = jnp.zeros((48, 1536), F32)
    for z in range(8):
        base = 160 * z // 128 * 128
        off = 160 * z - base
        tail = pieces[z, 80:, :].astype(F32)
        tail = jnp.concatenate([tail] + [pltpu.roll(tail, 128 - 32 * i, 1) for i in (1, 2)], axis=0)
        value = jnp.concatenate(
            [pieces[z, :48, :].astype(F32), tail, jnp.zeros((48, 128), F32)], axis=1
        )
        if off:
            value = pltpu.roll(value, off, 1)
        wide[:, base : base + 384] = jnp.where(
            (lane >= off) & (lane < off + 160), value, wide[:, base : base + 384]
        )
    image_out[...] = wide[:, :1280].astype(BF16)


def exchanged(array, axes):
    return lax.all_to_all(array, axes, split_axis=0, concat_axis=0, tiled=True)


def swapped(array):
    return lax.ppermute(array, "core", [(0, 1), (1, 0)])


def local(image, filter_one, filter_two, cotangent):
    scale = 1.0 / math.sqrt(48 * 1280)
    yh, z, yl, x, core = (lax.axis_index(a) for a in AXES)
    at = jnp.stack([yh, z, 2 * yh + yl, x, core]).astype(jnp.int32)

    def rows_first(a):
        return jnp.transpose(a, (1, 0, 2)).reshape(48, 1280)

    filters = [jnp.transpose(f, (1, 0, 2)).reshape(144, 16) for f in (filter_one, filter_two)]
    pieces = call(
        windows_kernel,
        shape((8, 64, 384)),
        [pltpu.VMEM((48, 1792), F32)] * 2
        + [pltpu.VMEM((48, 1280), BF16)] * 2
        + [pltpu.VMEM((144, 16), BF16)] * 2
        + [pltpu.SemaphoreType.DMA((4,))],
        [rows_first(image), rows_first(cotangent), *filters],
        at,
        space=pltpu.HBM,
    )
    pieces = call(
        turn_kernel,
        shape((16, 432, 128)),
        [pltpu.VMEM((384, 128), F32), pltpu.VMEM((48, 128), F32)],
        [exchanged(pieces, "z")],
        at,
    )
    pieces = exchanged(pieces, TORUS)
    send, keep, image_send, image_keep = call(
        conv_kernel,
        [shape((2, 8, 288, 128))] * 2 + [shape((2, 4, 48, 128))] * 2,
        [
            pltpu.VMEM((64, 48, 256), BF16),
            pltpu.VMEM((18, 16, 16, 256), BF16),
            pltpu.VMEM((40, W, 256), F32),
            pltpu.VMEM((40, W, 256), BF16),
            pltpu.VMEM((40, W, 256), BF16),
            pltpu.VMEM((40, W, 256), BF16),
            pltpu.VMEM((3, 40, 16, 256), BF16),
            pltpu.VMEM((2, 2, 8, 18, 16, 128), BF16),
            pltpu.VMEM((24, 16, 256), BF16),
        ],
        [pieces, swapped(pieces)],
        at,
        28,
    )
    pieces = call(
        scatter_kernel,
        shape((16, 336, 128)),
        [],
        [keep, swapped(send), image_keep, swapped(image_send)],
        at,
    )
    pieces = call(
        regroup_kernel,
        shape((8, 96, 128)),
        [pltpu.VMEM((256, 128), F32)],
        [exchanged(pieces, TORUS)],
        at,
    )
    image_grad, *filter_grads = call(
        functools.partial(finish_kernel, scale),
        [shape((48, 1280)), shape((144, 16), F32), shape((144, 16), F32)],
        [pltpu.VMEM((48, 1536), F32)],
        [exchanged(pieces, "z")],
        at,
    )
    grad_one, grad_two = (
        jnp.transpose(g.reshape(9, 16, 16), (1, 0, 2)) for g in filter_grads
    )
    return jnp.transpose(image_grad.reshape(3, 16, 1280), (1, 0, 2)), grad_one, grad_two


def solution(mesh):
    finer = Mesh(mesh.devices.reshape(2, 8, 2, 4, 2), AXES)
    return jax.shard_map(
        local,
        mesh=finer,
        in_specs=(
            P(CHAN, STRIP, None),
            P(STRIP, None, CHAN),
            P(STRIP, None, CHAN),
            P(CHAN, STRIP, None),
        ),
        out_specs=(P(CHAN, STRIP, None), P(STRIP, None, CHAN), P(STRIP, None, CHAN)),
        check_vma=False,
    )
```

```python
import functools
import math

import jax
import jax.numpy as jnp
from jax import lax
from jax.experimental import pallas as pl
from jax.experimental.pallas import tpu as pltpu
from jax.sharding import Mesh
from jax.sharding import PartitionSpec as P


AXES = ("yh", "z", "yl", "x", "core")
CHAN = ("yh", "z")
STRIP = ("yl", "x", "core")
TORUS = ("yh", "yl", "x")
F32 = jnp.float32
BF16 = jnp.bfloat16

W = 32


def call(kernel, outs, scratch, args, prefetch, room=10, space=None, cost=10**7):
    return pl.pallas_call(
        kernel,
        out_shape=outs,
        in_specs=[pl.BlockSpec(memory_space=pltpu.SMEM)]
        + [pl.BlockSpec(memory_space=s) for s in (space or [pltpu.VMEM] * len(args))],
        out_specs=jax.tree.map(lambda _: pl.BlockSpec(memory_space=pltpu.VMEM), outs),
        scratch_shapes=scratch,
        cost_estimate=pl.CostEstimate(flops=cost, bytes_accessed=10**6, transcendentals=0),
        compiler_params=pltpu.CompilerParams(vmem_limit_bytes=room * 2**20),
    )(prefetch, *args)


def shape(dims, kind=BF16):
    return jax.ShapeDtypeStruct(dims, kind)


def windows_kernel(at, *rest):
    sources, (windows, image_wide, cotangent_wide), held, arrived = (
        rest[:4],
        rest[4:7],
        rest[7:11],
        rest[11],
    )
    copies = [
        pltpu.make_async_copy(a, b, arrived.at[k]) for k, (a, b) in enumerate(zip(sources, held))
    ]
    for copy in copies:
        copy.start()
    for copy in copies:
        copy.wait()
    image, cotangent, filter_one, filter_two = held
    row = lax.broadcasted_iota(jnp.int32, (16, 16), 0)
    unit = (row == lax.broadcasted_iota(jnp.int32, (16, 16), 1)).astype(F32).astype(BF16)
    pieces = jnp.concatenate(
        [
            lax.dot_general(
                unit, f[...], (((1,), (1,)), ((), ())), preferred_element_type=F32
            )
            for f in (filter_one, filter_two)
        ]
        + [jnp.zeros((16, 96), F32)],
        axis=1,
    ).astype(BF16)
    for wide, source in ((image_wide, image), (cotangent_wide, cotangent)):
        wide[:, :256] = jnp.zeros((48, 256), F32)
        wide[:, 1536:] = jnp.zeros((48, 256), F32)
        wide[:, 256:1536] = source[...].astype(F32)
    lane = lax.broadcasted_iota(jnp.int32, (48, 384), 1)
    for z in range(8):
        first = 256 + 160 * z - 8
        base = first // 128 * 128
        left = pltpu.roll(image_wide[:, base : base + 384], 384 - (first - base), 1)
        second = 256 + 160 * z - 4 - 176
        base = second // 128 * 128
        right = pltpu.roll(cotangent_wide[:, base : base + 512], 512 - (second - base), 1)[:, :384]
        windows[z, :48, :] = jnp.where(lane < 176, left, right).astype(BF16)
        windows[z, 48:, :] = pieces


def turn_kernel(at, *rest):
    held, outs, later, turned, chunk = rest
    for i in range(3):
        turned[...] = held[:, 16 * i : 16 * i + 16, :].reshape(128, 384).astype(F32).T
        for j in range(16):
            chunk[:32, :] = turned[10 * j : 10 * j + 32, :]
            chunk[26:48, :] = turned[176 + 10 * j : 198 + 10 * j, :]
            outs[j, 48 * i : 48 * i + 48, :] = chunk[...].astype(BF16)
    filters = held[:, 48:, :].reshape(128, 384).astype(F32).T[:288].astype(BF16)
    for j in range(16):
        outs[j, 144:, :] = filters[:144]
        later[j] = filters[144:]


def sigmoid(v):
    return 0.5 + 0.5 * jnp.tanh(0.5 * v)


def tap(wide, i, j):
    return wide[3 * i + j].reshape(256, 256)


def ahead(source, wide, start, rows):
    band = jnp.concatenate(
        [source[pl.ds(start + 2 * i - 2, rows), :W, :] for i in range(3)], axis=-1
    ).reshape(rows * W, 768)
    total = None
    for j in range(3):
        weights = jnp.concatenate([tap(wide, i, j) for i in range(3)], axis=0)
        term = jnp.dot(band, weights, preferred_element_type=F32)
        if j != 1:
            term = pltpu.roll(term, (rows * W - 2 * (j - 1)) % (rows * W), 0)
        total = term if total is None else total + term
    return total.reshape(rows, W, 256)


def backward(source, wide, start, rows):
    band = jnp.concatenate(
        [source[pl.ds(start - 2 * i + 2, rows), :, :] for i in range(3)], axis=-1
    ).reshape(rows * W, 768)
    total = None
    for j in range(3):
        weights = jnp.concatenate([tap(wide, i, j) for i in range(3)], axis=1)
        term = lax.dot_general(
            band, weights, (((1,), (1,)), ((), ())), preferred_element_type=F32
        )
        if j != 1:
            term = pltpu.roll(term, (rows * W + 2 * (j - 1)) % (rows * W), 0)
        total = term if total is None else total + term
    return total.reshape(rows, W, 256)


def slope(v):
    s = sigmoid(v)
    return s * (1.0 + v * (1.0 - s))


def each(start, count, rows, body):
    def step(k, _):
        body(start + k * rows)
        return 0

    lax.fori_loop(0, count, step, 0)


def cleared(at, target):
    z, y, x, core = (at[k] for k in range(1, 5))

    @pl.when(core == 0)
    def _():
        target[:8] = jnp.zeros((8, W, 256), BF16)

    @pl.when(core == 1)
    def _():
        target[32:] = jnp.zeros((8, W, 256), BF16)

    @pl.when((z == 0) & (y + x == 0))
    def _():
        target[:, :8, :] = jnp.zeros((40, 8, 256), BF16)

    @pl.when((z == 7) & (y + x == 6))
    def _():
        target[:, 18:, :] = jnp.zeros((40, 14, 256), BF16)


def first_kernel(at, own, other, acts, wide, pre, hidden):
    core = at[4]
    acts[:8] = jnp.zeros((8, 48, 256), BF16)
    acts[56:] = jnp.zeros((8, 48, 256), BF16)
    for pieces, side in ((own, core), (other, 1 - core)):
        for j in range(16):
            half = j // 8
            strip = 2 * (j % 8) + side
            lanes = slice(half * 128, half * 128 + 128)
            acts[pl.ds(3 * strip + 8, 3), :, lanes] = pieces[j, :144, :].reshape(3, 48, 128)
            wide[:, strip, :, lanes] = pieces[j, 144:, :].reshape(9, 16, 128)

    def first_step(start):
        value = ahead(acts, wide, start + 24 * core, 12)
        pre[pl.ds(start, 12)] = value
        hidden[pl.ds(start, 12)] = (value * sigmoid(value)).astype(BF16)

    each(2, 3, 12, first_step)
    cleared(at, hidden)


def conv_kernel(at, own, other, *rest):
    state, (send, keep, image_send, image_keep) = rest[:4], rest[4:8]
    wide, second, first, mine, terms, image_rows = rest[8:14]
    held, arrived = rest[14:18], rest[18]
    copies = [
        pltpu.make_async_copy(a, b, arrived.at[k]) for k, (a, b) in enumerate(zip(state, held))
    ]
    for copy in copies:
        copy.start()
    acts, wide_one, pre, hidden = held
    core = at[4]
    for pieces, side in ((own, core), (other, 1 - core)):
        for j in range(16):
            half = j // 8
            strip = 2 * (j % 8) + side
            wide[:, strip, :, half * 128 : half * 128 + 128] = pieces[j].reshape(9, 16, 128)

    for copy in copies:
        copy.wait()

    def second_step(start):
        rows = 16
        value = ahead(hidden, wide, start, rows)
        got = acts[pl.ds(start + 24 * core, rows), 16:, :].astype(F32).reshape(rows * W, 256)
        got = pltpu.roll(got, rows * W - 6, 0).reshape(rows, W, 256)
        second[pl.ds(start, rows)] = (got * slope(value)).astype(BF16)

    each(4, 2, 16, second_step)
    cleared(at, second)

    def third_step(start):
        rows = 14
        value = backward(second, wide, start, rows)
        first[pl.ds(start, rows)] = (value * slope(pre[pl.ds(start, rows)])).astype(BF16)

    each(6, 2, 14, third_step)
    cleared(at, first)

    def fourth_step(start):
        rows = 12
        value = backward(first, wide_one, start, rows)
        image_rows[pl.ds(start - 8, rows)] = value[:, 8:24, :].astype(BF16)

    each(8, 2, 12, fourth_step)
    for side, out in ((1 - core, image_send), (core, image_keep)):
        for k in range(4):
            for half in range(2):
                out[half, k] = image_rows[
                    pl.ds(6 * k + 3 * side, 3), :, 128 * half : 128 * half + 128
                ].reshape(48, 128)

    def narrowed(values, rows, shift):
        flat = values.astype(F32).reshape(rows * W, 256)
        flat = pltpu.roll(flat, (rows * W + shift) % (rows * W), 0)
        return flat.reshape(rows, W, 256)[:, :16, :]

    def weight_terms(values, grads, which):
        turned = narrowed(values, 28, -6).reshape(28 * 16, 256).T.astype(BF16)
        column = lax.broadcasted_iota(jnp.int32, (24, 16, 256), 1)
        for j in range(3):
            kept = (column >= 2 * j) & (column < 2 * j + 10)
            shifted = narrowed(grads[8:32], 24, 2 * j - 8)
            mine[j, 8:32] = jnp.where(kept, shifted, 0.0).astype(BF16)

        def step(i, _):
            for j in range(3):
                rows = mine[j, pl.ds(8 - 2 * i, 28)].reshape(28 * 16, 256)
                got = jnp.dot(turned, rows, preferred_element_type=F32).astype(BF16)
                got = got.reshape(8, 2, 16, 256)
                for side in range(2):
                    for half in range(2):
                        terms[side, half, :, 9 * which + 3 * i + j] = got[
                            :, side, :, 128 * half : 128 * half + 128
                        ]
            return 0

        lax.fori_loop(0, 3, step, 0)

    for j in range(3):
        mine[j, :8] = jnp.zeros((8, 16, 256), BF16)
        mine[j, 32:] = jnp.zeros((8, 16, 256), BF16)
    weight_terms(hidden[6:34], second, 1)
    weight_terms(acts[pl.ds(6 + 24 * core, 28), :W, :], first, 0)
    send[...] = terms[1 - core].reshape(2, 8, 288, 128)
    keep[...] = terms[core].reshape(2, 8, 288, 128)


def scatter_kernel(at, keep, got, image_keep, image_got, outs):
    for j in range(16):
        half, q = j // 8, j % 8
        outs[j, :288, :] = (keep[half, q].astype(F32) + got[half, q].astype(F32)).astype(BF16)
    for half in range(2):
        for k in range(4):
            outs[8 * half + 4 * at[4] + k, 288:, :] = image_keep[half, k]
            outs[8 * half + 4 - 4 * at[4] + k, 288:, :] = image_got[half, k]


def regroup_kernel(at, *rest):
    pieces, windows, columns = rest
    total = None
    for j in range(16):
        term = pieces[j, :288, :].astype(F32)
        total = term if total is None else total + term
    total = jnp.concatenate([total, jnp.zeros((96, 128), F32)], axis=0).T
    for z in range(8):
        windows[z, 48:64, :] = total[16 * z : 16 * z + 16, :128].astype(BF16)
        windows[z, 64:80, :] = total[16 * z : 16 * z + 16, 128:256].astype(BF16)
    lane = lax.broadcasted_iota(jnp.int32, (128, 128), 1)
    rest = pltpu.roll(total[:, 256:], 96, 1)
    columns[...] = jnp.zeros((256, 128), F32)
    for i in range(3):
        for j in range(16):
            columns[10 * j : 10 * j + 16, :] = pieces[j, 288 + 16 * i : 304 + 16 * i, :].astype(
                F32
            )
        turned = columns[...].T
        for z in range(8):
            windows[z, 16 * i : 16 * i + 16, :] = turned[16 * z : 16 * z + 16, :128].astype(BF16)
        end = turned[:, 128:]
        if i:
            end = pltpu.roll(end, 32 * i, 1)
        rest = jnp.where((lane >= 32 * i) & (lane < 32 * i + 32), end, rest)
    for z in range(8):
        windows[z, 80:, :] = rest[16 * z : 16 * z + 16].astype(BF16)


def finish_kernel(scale, at, pieces, image_out, grad_one, grad_two, wide):
    total = None
    for z in range(8):
        parts = [pieces[z, k : k + 16, :].astype(F32) for k in (48, 64, 80)]
        total = parts if total is None else [t + p for t, p in zip(total, parts)]
    total[2] = pltpu.roll(total[2], 32, 1)
    total = jnp.concatenate(total, axis=1) * scale
    for out, at_lane in ((grad_one, 0), (grad_two, 144)):
        part = total if at_lane == 0 else pltpu.roll(total, 384 - at_lane, 1)
        out[...] = jnp.concatenate([part[:, :256], jnp.zeros((112, 256), F32)], axis=0).T[:144, :16]
    lane = lax.broadcasted_iota(jnp.int32, (48, 384), 1)
    wide[...] = jnp.zeros((48, 1536), F32)
    for z in range(8):
        base = 160 * z // 128 * 128
        off = 160 * z - base
        tail = pieces[z, 80:, :].astype(F32)
        tail = jnp.concatenate([tail] + [pltpu.roll(tail, 128 - 32 * i, 1) for i in (1, 2)], axis=0)
        value = jnp.concatenate(
            [pieces[z, :48, :].astype(F32), tail, jnp.zeros((48, 128), F32)], axis=1
        )
        if off:
            value = pltpu.roll(value, off, 1)
        wide[:, base : base + 384] = jnp.where(
            (lane >= off) & (lane < off + 160), value, wide[:, base : base + 384]
        )
    image_out[...] = wide[:, :1280].astype(BF16)


def exchanged(array, axes):
    return lax.all_to_all(array, axes, split_axis=0, concat_axis=0, tiled=True)


def swapped(array):
    return lax.ppermute(array, "core", [(0, 1), (1, 0)])


def local(image, filter_one, filter_two, cotangent):
    scale = 1.0 / math.sqrt(48 * 1280)
    yh, z, yl, x, core = (lax.axis_index(a) for a in AXES)
    at = jnp.stack([yh, z, 2 * yh + yl, x, core]).astype(jnp.int32)

    def rows_first(a):
        return jnp.transpose(a, (1, 0, 2)).reshape(48, 1280)

    filters = [jnp.transpose(f, (1, 0, 2)).reshape(144, 16) for f in (filter_one, filter_two)]
    pieces = call(
        windows_kernel,
        shape((8, 64, 384)),
        [pltpu.VMEM((48, 1792), F32)] * 2
        + [pltpu.VMEM((48, 1280), BF16)] * 2
        + [pltpu.VMEM((144, 16), BF16)] * 2
        + [pltpu.SemaphoreType.DMA((4,))],
        [rows_first(image), rows_first(cotangent), *filters],
        at,
        room=63,
        space=[pltpu.HBM] * 4,
    )
    early, late = call(
        turn_kernel,
        [shape((16, 288, 128)), shape((16, 144, 128))],
        [pltpu.VMEM((384, 128), F32), pltpu.VMEM((48, 128), F32)],
        [exchanged(pieces, "z")],
        at,
    )
    early = exchanged(early, TORUS)
    late = exchanged(late, TORUS)
    early_other = swapped(early)
    state = call(
        first_kernel,
        [
            shape((64, 48, 256)),
            shape((9, 16, 16, 256)),
            shape((40, W, 256), F32),
            shape((40, W, 256)),
        ],
        [],
        [early, early_other],
        at,
        cost=2 * 10**9,
    )
    send, keep, image_send, image_keep = call(
        conv_kernel,
        [shape((2, 8, 288, 128))] * 2 + [shape((2, 4, 48, 128))] * 2,
        [
            pltpu.VMEM((9, 16, 16, 256), BF16),
            pltpu.VMEM((40, W, 256), BF16),
            pltpu.VMEM((40, W, 256), BF16),
            pltpu.VMEM((3, 40, 16, 256), BF16),
            pltpu.VMEM((2, 2, 8, 18, 16, 128), BF16),
            pltpu.VMEM((24, 16, 256), BF16),
            *(pltpu.VMEM(a.shape, a.dtype) for a in state),
            pltpu.SemaphoreType.DMA((4,)),
        ],
        [late, swapped(late), *(pltpu.with_memory_space_constraint(a, pltpu.HBM) for a in state)],
        at,
        room=24,
        space=[pltpu.VMEM] * 2 + [pltpu.HBM] * 4,
        cost=6 * 10**9,
    )
    pieces = call(
        scatter_kernel,
        shape((16, 336, 128)),
        [],
        [keep, swapped(send), image_keep, swapped(image_send)],
        at,
    )
    pieces = call(
        regroup_kernel,
        shape((8, 96, 128)),
        [pltpu.VMEM((256, 128), F32)],
        [exchanged(pieces, TORUS)],
        at,
    )
    image_grad, *filter_grads = call(
        functools.partial(finish_kernel, scale),
        [shape((48, 1280)), shape((144, 16), F32), shape((144, 16), F32)],
        [pltpu.VMEM((48, 1536), F32)],
        [exchanged(pieces, "z")],
        at,
    )
    grad_one, grad_two = (
        jnp.transpose(g.reshape(9, 16, 16), (1, 0, 2)) for g in filter_grads
    )
    return jnp.transpose(image_grad.reshape(3, 16, 1280), (1, 0, 2)), grad_one, grad_two


def solution(mesh):
    finer = Mesh(mesh.devices.reshape(2, 8, 2, 4, 2), AXES)
    return jax.shard_map(
        local,
        mesh=finer,
        in_specs=(
            P(CHAN, STRIP, None),
            P(STRIP, None, CHAN),
            P(STRIP, None, CHAN),
            P(CHAN, STRIP, None),
        ),
        out_specs=(P(CHAN, STRIP, None), P(STRIP, None, CHAN), P(STRIP, None, CHAN)),
        check_vma=False,
    )
```

```python
import functools
import math

import jax
import jax.numpy as jnp
from jax import lax
from jax.experimental import pallas as pl
from jax.experimental.pallas import tpu as pltpu
from jax.sharding import Mesh
from jax.sharding import PartitionSpec as P

AXES = ("yh", "z", "yl", "x", "core")
CHAN = ("yh", "z")
STRIP = ("yl", "x", "core")
TORUS = ("yh", "yl", "x")
F32 = jnp.float32
BF16 = jnp.bfloat16

W = 32


def call(kernel, outs, scratch, args, prefetch=None, room=10, space=pltpu.VMEM):
    where = [pl.BlockSpec(memory_space=space)] * len(args)
    if prefetch is not None:
        where = [pl.BlockSpec(memory_space=pltpu.SMEM)] + where
        args = [prefetch, *args]
    return pl.pallas_call(
        kernel,
        out_shape=outs,
        in_specs=where,
        out_specs=jax.tree.map(lambda _: pl.BlockSpec(memory_space=pltpu.VMEM), outs),
        scratch_shapes=scratch,
        compiler_params=pltpu.CompilerParams(vmem_limit_bytes=room * 2**20),
    )(*args)


def shape(dims, kind=BF16):
    return jax.ShapeDtypeStruct(dims, kind)


def windows_kernel(*rest):
    sources, (windows, image_wide, cotangent_wide), held, arrived = (
        rest[:4],
        rest[4:7],
        rest[7:11],
        rest[11],
    )
    copies = [
        pltpu.make_async_copy(a, b, arrived.at[k]) for k, (a, b) in enumerate(zip(sources, held))
    ]
    for copy in copies:
        copy.start()
    for copy in copies:
        copy.wait()
    image, cotangent, filter_one, filter_two = held
    row = lax.broadcasted_iota(jnp.int32, (16, 16), 0)
    unit = (row == lax.broadcasted_iota(jnp.int32, (16, 16), 1)).astype(F32).astype(BF16)
    pieces = jnp.concatenate(
        [
            lax.dot_general(
                unit, f[...], (((1,), (1,)), ((), ())), preferred_element_type=F32
            )
            for f in (filter_one, filter_two)
        ]
        + [jnp.zeros((16, 96), F32)],
        axis=1,
    ).astype(BF16)
    for wide, source in ((image_wide, image), (cotangent_wide, cotangent)):
        wide[:, :256] = jnp.zeros((48, 256), F32)
        wide[:, 1536:] = jnp.zeros((48, 256), F32)
        wide[:, 256:1536] = source[...].astype(F32)
    lane = lax.broadcasted_iota(jnp.int32, (48, 384), 1)
    for z in range(8):
        first = 256 + 160 * z - 8
        base = first // 128 * 128
        left = pltpu.roll(image_wide[:, base : base + 384], 384 - (first - base), 1)
        second = 256 + 160 * z - 4 - 176
        base = second // 128 * 128
        right = pltpu.roll(cotangent_wide[:, base : base + 512], 512 - (second - base), 1)[:, :384]
        windows[z, :48, :] = jnp.where(lane < 176, left, right).astype(BF16)
        windows[z, 48:, :] = pieces


def turn_kernel(*rest):
    held, outs, turned, chunk = rest
    for i in range(3):
        turned[...] = held[:, 16 * i : 16 * i + 16, :].reshape(128, 384).astype(F32).T
        for j in range(16):
            chunk[:32, :] = turned[10 * j : 10 * j + 32, :]
            chunk[26:48, :] = turned[176 + 10 * j : 198 + 10 * j, :]
            outs[j, 48 * i : 48 * i + 48, :] = chunk[...].astype(BF16)
    filters = held[:, 48:, :].reshape(128, 384).astype(F32).T[:288].astype(BF16)
    for j in range(16):
        outs[j, 144:, :] = filters


def sigmoid(v):
    return 0.5 + 0.5 * jnp.tanh(0.5 * v)


def rolled(value, shift):
    shift %= value.shape[0]
    return pltpu.roll(value, shift, 0) if shift else value


def tapped(band, wide, shifts, transposed):
    total = None
    for j in range(3):
        taps = [wide[3 * i + j].reshape(256, 256) for i in range(3)]
        weights = jnp.concatenate(taps, axis=1 if transposed else 0)
        over = (((1,), (1 if transposed else 0,)), ((), ()))
        term = lax.dot_general(band, weights, over, preferred_element_type=F32)
        term = rolled(term, shifts[j])
        total = term if total is None else total + term
    return total


def silu_slope(v):
    s = sigmoid(v)
    return s * (1.0 + v * (1.0 - s))


def conv_kernel(at, *rest):
    own, other = rest[:2]
    send, keep, image_send, image_keep = rest[2:6]
    acts, wides, pre, hidden, second, first, mine, terms, image_rows = rest[6:]
    z, y, x, core = (at[k] for k in range(1, 5))
    acts[:8] = jnp.zeros((8, 48, 256), BF16)
    acts[56:] = jnp.zeros((8, 48, 256), BF16)
    for pieces, side in ((own, core), (other, 1 - core)):
        for j in range(16):
            half = j // 8
            strip = 2 * (j % 8) + side
            lanes = slice(half * 128, half * 128 + 128)
            acts[pl.ds(3 * strip + 8, 3), :, lanes] = pieces[j, :144, :].reshape(3, 48, 128)
            wides[:, strip, :, lanes] = pieces[j, 144:, :].reshape(18, 16, 128)
    wide_one, wide_two = wides.at[:9], wides.at[9:]

    rows_out = 32 * core
    hidden[pl.ds(pl.multiple_of(24 * rows_out, 48), 192)] = jnp.zeros((192, 256), BF16)
    second[pl.ds(pl.multiple_of(24 * rows_out, 48), 192)] = jnp.zeros((192, 256), BF16)
    first[pl.ds(rows_out, 8)] = jnp.zeros((8, 16, 256), BF16)
    left = 160 * z + 10 * (4 * y + x) - 8

    def mask(begin, columns):
        c = lax.broadcasted_iota(jnp.int32, (1, columns, 256), 1) + (left + begin)
        return ((c >= 0) & (c < 1280)).astype(F32)

    def flat(start, rows):
        return pl.ds(pl.multiple_of(start * 24, 48), rows * 24)

    mask_24, mask_16 = mask(2, 24), mask(6, 16)

    for k in range(2):
        rows = (16, 14)[k]
        start = 8 - 6 * core + 16 * k
        band = jnp.concatenate(
            [acts[pl.ds(start + 24 * core + 2 * i - 2, rows), :W, :] for i in range(3)], axis=-1
        ).reshape(rows * W, 768)
        value = tapped(band, wide_one, (0, -2, -4), False)
        pre[pl.ds(start, rows)] = rolled(value, -4).reshape(rows, W, 256)[:, :16, :]
        value = value.reshape(rows, W, 256)[:, :24, :]
        value = value * sigmoid(value) * mask_24
        hidden[flat(start, rows)] = value.reshape(rows * 24, 256).astype(BF16)

    def second_step(k, _):
        rows = 14
        start = 8 - 4 * core + rows * k
        band = jnp.concatenate([hidden[flat(start + 2 * i - 2, rows)] for i in range(3)], axis=-1)
        value = tapped(band, wide_two, (2, 0, -2), False).reshape(rows, 24, 256)
        got = acts[pl.ds(start + 24 * core, rows), 16:, :].astype(F32)[:, 8:, :]
        value = got * silu_slope(value) * mask_24
        second[flat(start, rows)] = value.reshape(rows * 24, 256).astype(BF16)
        return 0

    lax.fori_loop(0, 2, second_step, 0)

    start = 8 - 2 * core
    band = jnp.concatenate([second[flat(start - 2 * i + 2, 26)] for i in range(3)], axis=-1)
    value = tapped(band, wide_two, (-6, -4, -2), True).reshape(26, 24, 256)[:, :16, :]
    value = value * silu_slope(pre[pl.ds(start, 26)]) * mask_16
    first[pl.ds(start, 26)] = value.astype(BF16)

    band = jnp.concatenate([first[10 - 2 * i : 34 - 2 * i] for i in range(3)], axis=-1)
    value = tapped(band.reshape(384, 768), wide_one, (-4, -2, 0), True)
    image_rows[...] = value.reshape(24, 16, 256).astype(BF16)
    for side, out in ((1 - core, image_send), (core, image_keep)):
        for k in range(4):
            for half in range(2):
                out[half, k] = image_rows[
                    pl.ds(6 * k + 3 * side, 3), :, 128 * half : 128 * half + 128
                ].reshape(48, 128)

    def narrowed(values, columns, shift):
        rows = values.shape[0] // columns
        return rolled(values.astype(F32), shift).reshape(rows, columns, 256)[:, :16, :]

    def weight_terms(values, grads, columns, which):
        turned = values.reshape(28 * 16, 256).T.astype(BF16)
        column = lax.broadcasted_iota(jnp.int32, (24, 16, 256), 1)
        for j in range(3):
            kept = (column >= 2 * j) & (column < 2 * j + 10)
            shifted = narrowed(grads, columns, 2 * j - 2 - (4 if columns == 24 else 0))
            mine[j, 8:32] = jnp.where(kept, shifted, 0.0).astype(BF16)

        def step(i, _):
            for j in range(3):
                rows = mine[j, pl.ds(8 - 2 * i, 28)].reshape(28 * 16, 256)
                got = jnp.dot(turned, rows, preferred_element_type=F32).astype(BF16)
                got = got.reshape(8, 2, 16, 256)
                for side in range(2):
                    for half in range(2):
                        terms[side, half, :, 9 * which + 3 * i + j] = got[
                            :, side, :, 128 * half : 128 * half + 128
                        ]
            return 0

        lax.fori_loop(0, 3, step, 0)

    for j in range(3):
        mine[j, :8] = jnp.zeros((8, 16, 256), BF16)
        mine[j, 32:] = jnp.zeros((8, 16, 256), BF16)
    weight_terms(narrowed(hidden[144:816], 24, -4), second[192:768], 24, 1)
    image_band = acts[pl.ds(6 + 24 * core, 28), :W, :].reshape(28 * W, 256)
    weight_terms(narrowed(image_band, W, -6), first[8:32].reshape(24 * 16, 256), 16, 0)
    send[...] = terms[1 - core].reshape(2, 8, 288, 128)
    keep[...] = terms[core].reshape(2, 8, 288, 128)


def scatter_kernel(at, keep, got, image_keep, image_got, outs):
    for j in range(16):
        half, q = j // 8, j % 8
        outs[j, :288, :] = (keep[half, q].astype(F32) + got[half, q].astype(F32)).astype(BF16)
    for half in range(2):
        for k in range(4):
            outs[8 * half + 4 * at[4] + k, 288:, :] = image_keep[half, k]
            outs[8 * half + 4 - 4 * at[4] + k, 288:, :] = image_got[half, k]


def regroup_kernel(*rest):
    pieces, windows, columns = rest
    total = None
    for j in range(16):
        term = pieces[j, :288, :].astype(F32)
        total = term if total is None else total + term
    total = jnp.concatenate([total, jnp.zeros((96, 128), F32)], axis=0).T
    for z in range(8):
        windows[z, 48:64, :] = total[16 * z : 16 * z + 16, :128].astype(BF16)
        windows[z, 64:80, :] = total[16 * z : 16 * z + 16, 128:256].astype(BF16)
    lane = lax.broadcasted_iota(jnp.int32, (128, 128), 1)
    rest = pltpu.roll(total[:, 256:], 96, 1)
    columns[...] = jnp.zeros((256, 128), F32)
    for i in range(3):
        for j in range(16):
            columns[10 * j : 10 * j + 16, :] = pieces[j, 288 + 16 * i : 304 + 16 * i, :].astype(
                F32
            )
        turned = columns[...].T
        for z in range(8):
            windows[z, 16 * i : 16 * i + 16, :] = turned[16 * z : 16 * z + 16, :128].astype(BF16)
        end = turned[:, 128:]
        if i:
            end = pltpu.roll(end, 32 * i, 1)
        rest = jnp.where((lane >= 32 * i) & (lane < 32 * i + 32), end, rest)
    for z in range(8):
        windows[z, 80:, :] = rest[16 * z : 16 * z + 16].astype(BF16)


def finish_kernel(scale, pieces, image_out, grad_one, grad_two, wide):
    total = None
    for z in range(8):
        parts = [pieces[z, k : k + 16, :].astype(F32) for k in (48, 64, 80)]
        total = parts if total is None else [t + p for t, p in zip(total, parts)]
    total[2] = pltpu.roll(total[2], 32, 1)
    total = jnp.concatenate(total, axis=1) * scale
    for out, at_lane in ((grad_one, 0), (grad_two, 144)):
        part = total if at_lane == 0 else pltpu.roll(total, 384 - at_lane, 1)
        out[...] = jnp.concatenate([part[:, :256], jnp.zeros((112, 256), F32)], axis=0).T[:144, :16]
    lane = lax.broadcasted_iota(jnp.int32, (48, 384), 1)
    wide[...] = jnp.zeros((48, 1536), F32)
    for z in range(8):
        base = 160 * z // 128 * 128
        off = 160 * z - base
        tail = pieces[z, 80:, :].astype(F32)
        tail = jnp.concatenate([tail] + [pltpu.roll(tail, 128 - 32 * i, 1) for i in (1, 2)], axis=0)
        value = jnp.concatenate(
            [pieces[z, :48, :].astype(F32), tail, jnp.zeros((48, 128), F32)], axis=1
        )
        if off:
            value = pltpu.roll(value, off, 1)
        wide[:, base : base + 384] = jnp.where(
            (lane >= off) & (lane < off + 160), value, wide[:, base : base + 384]
        )
    image_out[...] = wide[:, :1280].astype(BF16)


def exchanged(array, axes):
    return lax.all_to_all(array, axes, split_axis=0, concat_axis=0, tiled=True)


def swapped(array):
    return lax.ppermute(array, "core", [(0, 1), (1, 0)])


def local(image, filter_one, filter_two, cotangent):
    scale = 1.0 / math.sqrt(48 * 1280)
    yh, z, yl, x, core = (lax.axis_index(a) for a in AXES)
    at = jnp.stack([yh, z, 2 * yh + yl, x, core]).astype(jnp.int32)

    def rows_first(a):
        return jnp.transpose(a, (1, 0, 2)).reshape(48, 1280)

    filters = [jnp.transpose(f, (1, 0, 2)).reshape(144, 16) for f in (filter_one, filter_two)]
    pieces = call(
        windows_kernel,
        shape((8, 64, 384)),
        [pltpu.VMEM((48, 1792), F32)] * 2
        + [pltpu.VMEM((48, 1280), BF16)] * 2
        + [pltpu.VMEM((144, 16), BF16)] * 2
        + [pltpu.SemaphoreType.DMA((4,))],
        [rows_first(image), rows_first(cotangent), *filters],
        room=63,
        space=pltpu.HBM,
    )
    pieces = call(
        turn_kernel,
        shape((16, 432, 128)),
        [pltpu.VMEM((384, 128), F32), pltpu.VMEM((48, 128), F32)],
        [exchanged(pieces, "z")],
    )
    pieces = exchanged(pieces, TORUS)
    send, keep, image_send, image_keep = call(
        conv_kernel,
        [shape((2, 8, 288, 128))] * 2 + [shape((2, 4, 48, 128))] * 2,
        [
            pltpu.VMEM((64, 48, 256), BF16),
            pltpu.VMEM((18, 16, 16, 256), BF16),
            pltpu.VMEM((40, 16, 256), F32),
            pltpu.VMEM((40 * 24, 256), BF16),
            pltpu.VMEM((40 * 24, 256), BF16),
            pltpu.VMEM((40, 16, 256), BF16),
            pltpu.VMEM((3, 40, 16, 256), BF16),
            pltpu.VMEM((2, 2, 8, 18, 16, 128), BF16),
            pltpu.VMEM((24, 16, 256), BF16),
        ],
        [pieces, swapped(pieces)],
        at,
        28,
    )
    pieces = call(
        scatter_kernel,
        shape((16, 336, 128)),
        [],
        [keep, swapped(send), image_keep, swapped(image_send)],
        at,
    )
    pieces = call(
        regroup_kernel,
        shape((8, 96, 128)),
        [pltpu.VMEM((256, 128), F32)],
        [exchanged(pieces, TORUS)],
    )
    image_grad, *filter_grads = call(
        functools.partial(finish_kernel, scale),
        [shape((48, 1280)), shape((144, 16), F32), shape((144, 16), F32)],
        [pltpu.VMEM((48, 1536), F32)],
        [exchanged(pieces, "z")],
    )
    grad_one, grad_two = (
        jnp.transpose(g.reshape(9, 16, 16), (1, 0, 2)) for g in filter_grads
    )
    return jnp.transpose(image_grad.reshape(3, 16, 1280), (1, 0, 2)), grad_one, grad_two


def solution(mesh):
    finer = Mesh(mesh.devices.reshape(2, 8, 2, 4, 2), AXES)
    return jax.shard_map(
        local,
        mesh=finer,
        in_specs=(
            P(CHAN, STRIP, None),
            P(STRIP, None, CHAN),
            P(STRIP, None, CHAN),
            P(CHAN, STRIP, None),
        ),
        out_specs=(P(CHAN, STRIP, None), P(STRIP, None, CHAN), P(STRIP, None, CHAN)),
        check_vma=False,
    )
```

```python
import functools
import math

import jax
import jax.numpy as jnp
from jax import lax
from jax.experimental import pallas as pl
from jax.experimental.pallas import tpu as pltpu
from jax.sharding import Mesh
from jax.sharding import PartitionSpec as P

AXES = ("yh", "z", "yl", "x", "core")
CHAN = ("yh", "z")
STRIP = ("yl", "x", "core")
TORUS = ("yh", "yl", "x")
F32 = jnp.float32
BF16 = jnp.bfloat16

W = 32


def call(kernel, outs, scratch, args, room=10, space=pltpu.VMEM):
    return pl.pallas_call(
        kernel,
        out_shape=outs,
        in_specs=[pl.BlockSpec(memory_space=space)] * len(args),
        out_specs=jax.tree.map(lambda _: pl.BlockSpec(memory_space=pltpu.VMEM), outs),
        scratch_shapes=scratch,
        compiler_params=pltpu.CompilerParams(vmem_limit_bytes=room * 2**20),
    )(*args)


def shape(dims, kind=BF16):
    return jax.ShapeDtypeStruct(dims, kind)


def windows_kernel(*rest):
    sources, (windows, image_wide, cotangent_wide), held, arrived = (
        rest[:4],
        rest[4:7],
        rest[7:11],
        rest[11],
    )
    copies = [
        pltpu.make_async_copy(a, b, arrived.at[k]) for k, (a, b) in enumerate(zip(sources, held))
    ]
    for copy in copies:
        copy.start()
    for copy in copies:
        copy.wait()
    image, cotangent, filter_one, filter_two = held
    row = lax.broadcasted_iota(jnp.int32, (16, 16), 0)
    unit = (row == lax.broadcasted_iota(jnp.int32, (16, 16), 1)).astype(F32).astype(BF16)
    pieces = jnp.concatenate(
        [
            lax.dot_general(
                unit, f[...], (((1,), (1,)), ((), ())), preferred_element_type=F32
            )
            for f in (filter_one, filter_two)
        ]
        + [jnp.zeros((16, 96), F32)],
        axis=1,
    )
    ends = pltpu.roll(pieces[:, 256:], 88, 1)
    ends = jnp.concatenate([ends, ends, ends], axis=0)
    for wide, source in ((image_wide, image), (cotangent_wide, cotangent)):
        wide[:, :256] = jnp.zeros((48, 256), F32)
        wide[:, 1536:] = jnp.zeros((48, 256), F32)
        wide[:, 256:1536] = source[...].astype(F32)
    lane = lax.broadcasted_iota(jnp.int32, (48, 384), 1)
    for z in range(8):
        first = 256 + 160 * z - 8
        base = first // 128 * 128
        left = pltpu.roll(image_wide[:, base : base + 384], 384 - (first - base), 1)
        second = 256 + 160 * z - 4 - 176
        base = second // 128 * 128
        right = pltpu.roll(cotangent_wide[:, base : base + 512], 512 - (second - base), 1)[:, :384]
        both = jnp.where(lane < 176, left, right)
        windows[z, :48, :] = both[:, :128].astype(BF16)
        windows[z, 48:96, :] = both[:, 128:256].astype(BF16)
        windows[z, 96:144, :] = jnp.where(lane[:, :128] < 88, both[:, 256:], ends).astype(BF16)
        windows[z, 144:160, :] = pieces[:, :128].astype(BF16)
        windows[z, 160:, :] = pieces[:, 128:256].astype(BF16)


def turn_kernel(*rest):
    held, outs, turned, chunk = rest
    for i in range(3):
        parts = [held[:, k + 16 * i : k + 16 * i + 16, :].reshape(128, 128) for k in (0, 48, 96)]
        turned[...] = jnp.concatenate(parts, axis=1).astype(F32).T
        for j in range(16):
            chunk[:32, :] = turned[10 * j : 10 * j + 32, :]
            chunk[26:48, :] = turned[176 + 10 * j : 198 + 10 * j, :]
            outs[j, 48 * i : 48 * i + 48, :] = chunk[...].astype(BF16)
    parts = [held[:, k : k + 16, :].reshape(128, 128).astype(F32) for k in (144, 160, 96)]
    parts[2] = pltpu.roll(parts[2], 40, 1)
    filters = jnp.concatenate(parts, axis=1).T[:288].astype(BF16)
    for j in range(16):
        outs[j, 144:, :] = filters


def sigmoid(v):
    return 0.5 + 0.5 * jnp.tanh(0.5 * v)


def rolled(value, shift):
    shift %= value.shape[0]
    return pltpu.roll(value, shift, 0) if shift else value


def tapped(band, wide, shifts, transposed):
    total = None
    for j in range(3):
        taps = [wide[3 * i + j].reshape(256, 256) for i in range(3)]
        weights = jnp.concatenate(taps, axis=1 if transposed else 0)
        over = (((1,), (1 if transposed else 0,)), ((), ()))
        term = lax.dot_general(band, weights, over, preferred_element_type=F32)
        term = rolled(term, shifts[j])
        total = term if total is None else total + term
    return total


def silu_slope(v):
    s = sigmoid(v)
    return s * (1.0 + v * (1.0 - s))


def conv_kernel(*rest):
    own, other = rest[:2]
    send, keep, image_send, image_keep = rest[2:6]
    acts, wides, pre, hidden, second, first, mine, terms, image_rows, packed = rest[6:]
    yh, z, yl, x, core = (lax.axis_index(a) for a in AXES)
    y = 2 * yh + yl
    acts[:8] = jnp.zeros((8, 48, 256), BF16)
    acts[56:] = jnp.zeros((8, 48, 256), BF16)
    for pieces, side in ((own, core), (other, 1 - core)):
        for j in range(16):
            half = j // 8
            strip = 2 * (j % 8) + side
            lanes = slice(half * 128, half * 128 + 128)
            acts[pl.ds(3 * strip + 8, 3), :, lanes] = pieces[j, :144, :].reshape(3, 48, 128)
            wides[:, strip, :, lanes] = pieces[j, 144:, :].reshape(18, 16, 128)
    wide_one, wide_two = wides.at[:9], wides.at[9:]

    rows_out = 32 * core
    hidden[pl.ds(pl.multiple_of(24 * rows_out, 48), 192)] = jnp.zeros((192, 256), BF16)
    second[pl.ds(pl.multiple_of(24 * rows_out, 48), 192)] = jnp.zeros((192, 256), BF16)
    first[pl.ds(rows_out, 8)] = jnp.zeros((8, 16, 256), BF16)
    left = 160 * z + 10 * (4 * y + x) - 8

    def mask(begin, columns):
        c = lax.broadcasted_iota(jnp.int32, (1, columns, 256), 1) + (left + begin)
        return ((c >= 0) & (c < 1280)).astype(F32)

    def flat(start, rows):
        return pl.ds(pl.multiple_of(start * 24, 48), rows * 24)

    mask_24, mask_16 = mask(2, 24), mask(6, 16)

    for k in range(2):
        rows = (16, 14)[k]
        start = 8 - 6 * core + 16 * k
        band = jnp.concatenate(
            [acts[pl.ds(start + 24 * core + 2 * i - 2, rows), :W, :] for i in range(3)], axis=-1
        ).reshape(rows * W, 768)
        value = tapped(band, wide_one, (0, -2, -4), False)
        pre[pl.ds(start, rows)] = rolled(value, -4).reshape(rows, W, 256)[:, :16, :]
        value = value.reshape(rows, W, 256)[:, :24, :]
        value = value * sigmoid(value) * mask_24
        hidden[flat(start, rows)] = value.reshape(rows * 24, 256).astype(BF16)

    start = 8 - 4 * core
    band = jnp.concatenate([hidden[flat(start + 2 * i - 2, 28)] for i in range(3)], axis=-1)
    value = tapped(band, wide_two, (2, 0, -2), False).reshape(28, 24, 256)
    got = acts[pl.ds(start + 24 * core, 28), 16:, :].astype(F32)[:, 8:, :]
    value = got * silu_slope(value) * mask_24
    second[flat(start, 28)] = value.reshape(28 * 24, 256).astype(BF16)

    start = 8 - 2 * core
    band = jnp.concatenate([second[flat(start - 2 * i + 2, 26)] for i in range(3)], axis=-1)
    value = tapped(band, wide_two, (-6, -4, -2), True).reshape(26, 24, 256)[:, :16, :]
    value = value * silu_slope(pre[pl.ds(start, 26)]) * mask_16
    first[pl.ds(start, 26)] = value.astype(BF16)

    band = jnp.concatenate([first[10 - 2 * i : 34 - 2 * i] for i in range(3)], axis=-1)
    value = tapped(band.reshape(384, 768), wide_one, (-4, -2, 0), True)
    image_rows[...] = value.reshape(24, 16, 256)
    for side, out in ((1 - core, image_send), (core, image_keep)):
        for k in range(4):
            for half in range(2):
                lines = image_rows[pl.ds(6 * k + 3 * side, 3), :, 128 * half : 128 * half + 128]
                for i in range(3):
                    packed[10 * i : 10 * i + 16, :] = lines[i]
                out[half, k] = packed[:32, :].astype(BF16)

    def narrowed(values, columns, shift):
        rows = values.shape[0] // columns
        return rolled(values.astype(F32), shift).reshape(rows, columns, 256)[:, :16, :]

    def weight_terms(values, grads, columns, which):
        turned = values.reshape(28 * 16, 256).T.astype(BF16)
        column = lax.broadcasted_iota(jnp.int32, (24, 16, 256), 1)
        for j in range(3):
            kept = (column >= 2 * j) & (column < 2 * j + 10)
            shifted = narrowed(grads, columns, 2 * j - 2 - (4 if columns == 24 else 0))
            mine[j, 8:32] = jnp.where(kept, shifted, 0.0).astype(BF16)

        def step(i, _):
            for j in range(3):
                rows = mine[j, pl.ds(8 - 2 * i, 28)].reshape(28 * 16, 256)
                got = jnp.dot(turned, rows, preferred_element_type=F32).astype(BF16)
                got = got.reshape(8, 2, 16, 256)
                for side in range(2):
                    for half in range(2):
                        terms[side, half, :, 9 * which + 3 * i + j] = got[
                            :, side, :, 128 * half : 128 * half + 128
                        ]
            return 0

        lax.fori_loop(0, 3, step, 0)

    for j in range(3):
        mine[j, :8] = jnp.zeros((8, 16, 256), BF16)
        mine[j, 32:] = jnp.zeros((8, 16, 256), BF16)
    weight_terms(narrowed(hidden[144:816], 24, -4), second[192:768], 24, 1)
    image_band = acts[pl.ds(6 + 24 * core, 28), :W, :].reshape(28 * W, 256)
    weight_terms(narrowed(image_band, W, -6), first[8:32].reshape(24 * 16, 256), 16, 0)
    send[...] = terms[1 - core].reshape(2, 8, 288, 128)
    keep[...] = terms[core].reshape(2, 8, 288, 128)


def scatter_kernel(keep, got, image_keep, image_got, outs):
    core = lax.axis_index("core")
    for j in range(16):
        half, q = j // 8, j % 8
        outs[j, :288, :] = (keep[half, q].astype(F32) + got[half, q].astype(F32)).astype(BF16)
    for half in range(2):
        for k in range(4):
            outs[8 * half + 4 * core + k, 288:, :] = image_keep[half, k]
            outs[8 * half + 4 - 4 * core + k, 288:, :] = image_got[half, k]


def regroup_kernel(*rest):
    pieces, windows, columns, unpacked = rest
    unpacked[...] = pieces[:, 288:, :].astype(F32)
    total = None
    for j in range(16):
        term = pieces[j, :288, :].astype(F32)
        total = term if total is None else total + term
    total = jnp.concatenate([total, jnp.zeros((96, 128), F32)], axis=0).T
    for z in range(8):
        windows[z, 48:64, :] = total[16 * z : 16 * z + 16, :128].astype(BF16)
        windows[z, 64:80, :] = total[16 * z : 16 * z + 16, 128:256].astype(BF16)
    lane = lax.broadcasted_iota(jnp.int32, (128, 128), 1)
    rest = pltpu.roll(total[:, 256:], 96, 1)
    columns[...] = jnp.zeros((256, 128), F32)
    for i in range(3):
        for j in range(16):
            columns[10 * j : 10 * j + 10, :] = unpacked[j, 10 * i : 10 * i + 10, :]
        turned = columns[...].T
        for z in range(8):
            windows[z, 16 * i : 16 * i + 16, :] = turned[16 * z : 16 * z + 16, :128].astype(BF16)
        end = turned[:, 128:]
        if i:
            end = pltpu.roll(end, 32 * i, 1)
        rest = jnp.where((lane >= 32 * i) & (lane < 32 * i + 32), end, rest)
    for z in range(8):
        windows[z, 80:, :] = rest[16 * z : 16 * z + 16].astype(BF16)


def finish_kernel(scale, pieces, image_out, grad_one, grad_two, wide):
    total = None
    for z in range(8):
        parts = [pieces[z, k : k + 16, :].astype(F32) for k in (48, 64, 80)]
        total = parts if total is None else [t + p for t, p in zip(total, parts)]
    total[2] = pltpu.roll(total[2], 32, 1)
    total = jnp.concatenate(total, axis=1) * scale
    for out, at_lane in ((grad_one, 0), (grad_two, 144)):
        part = total if at_lane == 0 else pltpu.roll(total, 384 - at_lane, 1)
        out[...] = jnp.concatenate([part[:, :256], jnp.zeros((112, 256), F32)], axis=0).T[:144, :16]
    lane = lax.broadcasted_iota(jnp.int32, (48, 384), 1)
    wide[...] = jnp.zeros((48, 1536), F32)
    for z in range(8):
        base = 160 * z // 128 * 128
        off = 160 * z - base
        tail = pieces[z, 80:, :].astype(F32)
        tail = jnp.concatenate([tail] + [pltpu.roll(tail, 128 - 32 * i, 1) for i in (1, 2)], axis=0)
        value = jnp.concatenate(
            [pieces[z, :48, :].astype(F32), tail, jnp.zeros((48, 128), F32)], axis=1
        )
        if off:
            value = pltpu.roll(value, off, 1)
        wide[:, base : base + 384] = jnp.where(
            (lane >= off) & (lane < off + 160), value, wide[:, base : base + 384]
        )
    image_out[...] = wide[:, :1280].astype(BF16)


def exchanged(array, axes):
    return lax.all_to_all(array, axes, split_axis=0, concat_axis=0, tiled=True)


def swapped(array):
    return lax.ppermute(array, "core", [(0, 1), (1, 0)])


def local(image, filter_one, filter_two, cotangent):
    scale = 1.0 / math.sqrt(48 * 1280)
    def rows_first(a):
        return jnp.transpose(a, (1, 0, 2)).reshape(48, 1280)

    filters = [jnp.transpose(f, (1, 0, 2)).reshape(144, 16) for f in (filter_one, filter_two)]
    pieces = call(
        windows_kernel,
        shape((8, 176, 128)),
        [pltpu.VMEM((48, 1792), F32)] * 2
        + [pltpu.VMEM((48, 1280), BF16)] * 2
        + [pltpu.VMEM((144, 16), BF16)] * 2
        + [pltpu.SemaphoreType.DMA((4,))],
        [rows_first(image), rows_first(cotangent), *filters],
        room=63,
        space=pltpu.HBM,
    )
    pieces = call(
        turn_kernel,
        shape((16, 432, 128)),
        [pltpu.VMEM((384, 128), F32), pltpu.VMEM((48, 128), F32)],
        [exchanged(pieces, "z")],
    )
    pieces = exchanged(pieces, TORUS)
    send, keep, image_send, image_keep = call(
        conv_kernel,
        [shape((2, 8, 288, 128))] * 2 + [shape((2, 4, 32, 128))] * 2,
        [
            pltpu.VMEM((64, 48, 256), BF16),
            pltpu.VMEM((18, 16, 16, 256), BF16),
            pltpu.VMEM((40, 16, 256), F32),
            pltpu.VMEM((40 * 24, 256), BF16),
            pltpu.VMEM((40 * 24, 256), BF16),
            pltpu.VMEM((40, 16, 256), BF16),
            pltpu.VMEM((3, 40, 16, 256), BF16),
            pltpu.VMEM((2, 2, 8, 18, 16, 128), BF16),
            pltpu.VMEM((24, 16, 256), F32),
            pltpu.VMEM((40, 128), F32),
        ],
        [pieces, swapped(pieces)],
        room=28,
    )
    pieces = call(
        scatter_kernel,
        shape((16, 320, 128)),
        [],
        [keep, swapped(send), image_keep, swapped(image_send)],
    )
    pieces = call(
        regroup_kernel,
        shape((8, 96, 128)),
        [pltpu.VMEM((256, 128), F32), pltpu.VMEM((16, 32, 128), F32)],
        [exchanged(pieces, TORUS)],
    )
    image_grad, *filter_grads = call(
        functools.partial(finish_kernel, scale),
        [shape((48, 1280)), shape((144, 16), F32), shape((144, 16), F32)],
        [pltpu.VMEM((48, 1536), F32)],
        [exchanged(pieces, "z")],
    )
    grad_one, grad_two = (
        jnp.transpose(g.reshape(9, 16, 16), (1, 0, 2)) for g in filter_grads
    )
    return jnp.transpose(image_grad.reshape(3, 16, 1280), (1, 0, 2)), grad_one, grad_two


def solution(mesh):
    finer = Mesh(mesh.devices.reshape(2, 8, 2, 4, 2), AXES)
    return jax.shard_map(
        local,
        mesh=finer,
        in_specs=(
            P(CHAN, STRIP, None),
            P(STRIP, None, CHAN),
            P(STRIP, None, CHAN),
            P(CHAN, STRIP, None),
        ),
        out_specs=(P(CHAN, STRIP, None), P(STRIP, None, CHAN), P(STRIP, None, CHAN)),
        check_vma=False,
    )
```

```python
import functools
import math

import jax
import jax.numpy as jnp
from jax import lax
from jax.experimental import pallas as pl
from jax.experimental.pallas import tpu as pltpu
from jax.sharding import Mesh
from jax.sharding import PartitionSpec as P

AXES = ("yh", "z", "yl", "x", "core")
CHAN = ("yh", "z")
STRIP = ("yl", "x", "core")
RING = [(y, x if y % 2 == 0 else 3 - x) for y in range(4) for x in range(4)]
TORUS = [
    [(((y // 2 * 8 + z) * 2 + y % 2) * 4 + x) * 2 + core for y, x in RING]
    for z in range(8)
    for core in range(2)
]
F32 = jnp.float32
BF16 = jnp.bfloat16

W = 32


def call(kernel, outs, scratch, args, room=10, space=pltpu.VMEM):
    return pl.pallas_call(
        kernel,
        out_shape=outs,
        in_specs=[pl.BlockSpec(memory_space=space)] * len(args),
        out_specs=jax.tree.map(lambda _: pl.BlockSpec(memory_space=pltpu.VMEM), outs),
        scratch_shapes=scratch,
        compiler_params=pltpu.CompilerParams(vmem_limit_bytes=room * 2**20),
    )(*args)


def shape(dims, kind=BF16):
    return jax.ShapeDtypeStruct(dims, kind)


def windows_kernel(*rest):
    sources, (windows, image_wide, cotangent_wide), held, arrived = (
        rest[:4],
        rest[4:7],
        rest[7:11],
        rest[11],
    )
    copies = [
        pltpu.make_async_copy(a, b, arrived.at[k]) for k, (a, b) in enumerate(zip(sources, held))
    ]
    for copy in copies:
        copy.start()
    for copy in copies:
        copy.wait()
    image, cotangent, filter_one, filter_two = held
    row = lax.broadcasted_iota(jnp.int32, (16, 16), 0)
    unit = (row == lax.broadcasted_iota(jnp.int32, (16, 16), 1)).astype(F32).astype(BF16)
    pieces = jnp.concatenate(
        [
            lax.dot_general(
                unit, f[...], (((1,), (1,)), ((), ())), preferred_element_type=F32
            )
            for f in (filter_one, filter_two)
        ]
        + [jnp.zeros((16, 96), F32)],
        axis=1,
    )
    ends = pltpu.roll(pieces[:, 256:], 88, 1)
    ends = jnp.concatenate([ends, ends, ends], axis=0)
    for wide, source in ((image_wide, image), (cotangent_wide, cotangent)):
        wide[:, :256] = jnp.zeros((48, 256), F32)
        wide[:, 1536:] = jnp.zeros((48, 256), F32)
        wide[:, 256:1536] = source[...].astype(F32)
    lane = lax.broadcasted_iota(jnp.int32, (48, 384), 1)
    for z in range(8):
        first = 256 + 160 * z - 8
        base = first // 128 * 128
        left = pltpu.roll(image_wide[:, base : base + 384], 384 - (first - base), 1)
        second = 256 + 160 * z - 4 - 176
        base = second // 128 * 128
        right = pltpu.roll(cotangent_wide[:, base : base + 512], 512 - (second - base), 1)[:, :384]
        both = jnp.where(lane < 176, left, right)
        windows[z, :48, :] = both[:, :128].astype(BF16)
        windows[z, 48:96, :] = both[:, 128:256].astype(BF16)
        windows[z, 96:144, :] = jnp.where(lane[:, :128] < 88, both[:, 256:], ends).astype(BF16)
        windows[z, 144:160, :] = pieces[:, :128].astype(BF16)
        windows[z, 160:, :] = pieces[:, 128:256].astype(BF16)


def turn_kernel(*rest):
    held, outs, turned, chunk = rest
    for i in range(3):
        parts = [held[:, k + 16 * i : k + 16 * i + 16, :].reshape(128, 128) for k in (0, 48, 96)]
        turned[...] = jnp.concatenate(parts, axis=1).astype(F32).T
        for j in range(16):
            chunk[:32, :] = turned[10 * j : 10 * j + 32, :]
            chunk[26:48, :] = turned[176 + 10 * j : 198 + 10 * j, :]
            outs[j, 48 * i : 48 * i + 48, :] = chunk[...].astype(BF16)
    parts = [held[:, k : k + 16, :].reshape(128, 128).astype(F32) for k in (144, 160, 96)]
    parts[2] = pltpu.roll(parts[2], 40, 1)
    filters = jnp.concatenate(parts, axis=1).T[:288].astype(BF16)
    for j in range(16):
        outs[j, 144:, :] = filters


def sigmoid(v):
    return 0.5 + 0.5 * jnp.tanh(0.5 * v)


def rolled(value, shift):
    shift %= value.shape[0]
    return pltpu.roll(value, shift, 0) if shift else value


def tapped(band, wide, shifts, transposed):
    total = None
    for j in range(3):
        taps = [wide[3 * i + j].reshape(256, 256) for i in range(3)]
        weights = jnp.concatenate(taps, axis=1 if transposed else 0)
        over = (((1,), (1 if transposed else 0,)), ((), ()))
        term = lax.dot_general(band, weights, over, preferred_element_type=F32)
        term = rolled(term, shifts[j])
        total = term if total is None else total + term
    return total


def silu_slope(v):
    s = sigmoid(v)
    return s * (1.0 + v * (1.0 - s))


def conv_kernel(*rest):
    own, other = rest[:2]
    send, keep, image_send, image_keep = rest[2:6]
    acts, wides, pre, hidden, second, first, mine, terms, image_rows, packed = rest[6:]
    yh, z, yl, x, core = (lax.axis_index(a) for a in AXES)
    y = 2 * yh + yl
    acts[:8] = jnp.zeros((8, 48, 256), BF16)
    acts[56:] = jnp.zeros((8, 48, 256), BF16)
    for pieces, side in ((own, core), (other, 1 - core)):
        for j, (at_y, at_x) in enumerate(RING):
            half = at_y // 2
            strip = 2 * (4 * (at_y % 2) + at_x) + side
            lanes = slice(half * 128, half * 128 + 128)
            acts[pl.ds(3 * strip + 8, 3), :, lanes] = pieces[j, :144, :].reshape(3, 48, 128)
            wides[:, strip, :, lanes] = pieces[j, 144:, :].reshape(18, 16, 128)
    wide_one, wide_two = wides.at[:9], wides.at[9:]

    rows_out = 32 * core
    hidden[pl.ds(pl.multiple_of(24 * rows_out, 48), 192)] = jnp.zeros((192, 256), BF16)
    second[pl.ds(pl.multiple_of(24 * rows_out, 48), 192)] = jnp.zeros((192, 256), BF16)
    first[pl.ds(rows_out, 8)] = jnp.zeros((8, 16, 256), BF16)
    left = 160 * z + 10 * (4 * y + jnp.where(yl == 0, x, 3 - x)) - 8

    def mask(begin, columns):
        c = lax.broadcasted_iota(jnp.int32, (1, columns, 256), 1) + (left + begin)
        return ((c >= 0) & (c < 1280)).astype(F32)

    def flat(start, rows):
        return pl.ds(pl.multiple_of(start * 24, 48), rows * 24)

    mask_24, mask_16 = mask(2, 24), mask(6, 16)

    for k in range(2):
        rows = (16, 14)[k]
        start = 8 - 6 * core + 16 * k
        band = jnp.concatenate(
            [acts[pl.ds(start + 24 * core + 2 * i - 2, rows), :W, :] for i in range(3)], axis=-1
        ).reshape(rows * W, 768)
        value = tapped(band, wide_one, (0, -2, -4), False)
        pre[pl.ds(start, rows)] = rolled(value, -4).reshape(rows, W, 256)[:, :16, :]
        value = value.reshape(rows, W, 256)[:, :24, :]
        value = value * sigmoid(value) * mask_24
        hidden[flat(start, rows)] = value.reshape(rows * 24, 256).astype(BF16)

    start = 8 - 4 * core
    band = jnp.concatenate([hidden[flat(start + 2 * i - 2, 28)] for i in range(3)], axis=-1)
    value = tapped(band, wide_two, (2, 0, -2), False).reshape(28, 24, 256)
    got = acts[pl.ds(start + 24 * core, 28), 16:, :].astype(F32)[:, 8:, :]
    value = got * silu_slope(value) * mask_24
    second[flat(start, 28)] = value.reshape(28 * 24, 256).astype(BF16)

    start = 8 - 2 * core
    band = jnp.concatenate([second[flat(start - 2 * i + 2, 26)] for i in range(3)], axis=-1)
    value = tapped(band, wide_two, (-6, -4, -2), True).reshape(26, 24, 256)[:, :16, :]
    value = value * silu_slope(pre[pl.ds(start, 26)]) * mask_16
    first[pl.ds(start, 26)] = value.astype(BF16)

    band = jnp.concatenate([first[10 - 2 * i : 34 - 2 * i] for i in range(3)], axis=-1)
    value = tapped(band.reshape(384, 768), wide_one, (-4, -2, 0), True)
    image_rows[...] = value.reshape(24, 16, 256)
    for side, out in ((1 - core, image_send), (core, image_keep)):
        for k in range(4):
            for half in range(2):
                lines = image_rows[pl.ds(6 * k + 3 * side, 3), :, 128 * half : 128 * half + 128]
                for i in range(3):
                    packed[10 * i : 10 * i + 16, :] = lines[i]
                out[half, k] = packed[:32, :].astype(BF16)

    def narrowed(values, columns, shift):
        rows = values.shape[0] // columns
        return rolled(values.astype(F32), shift).reshape(rows, columns, 256)[:, :16, :]

    def weight_terms(values, grads, columns, which):
        turned = values.reshape(28 * 16, 256).T.astype(BF16)
        column = lax.broadcasted_iota(jnp.int32, (24, 16, 256), 1)
        for j in range(3):
            kept = (column >= 2 * j) & (column < 2 * j + 10)
            shifted = narrowed(grads, columns, 2 * j - 2 - (4 if columns == 24 else 0))
            mine[j, 8:32] = jnp.where(kept, shifted, 0.0).astype(BF16)

        def step(i, _):
            for j in range(3):
                rows = mine[j, pl.ds(8 - 2 * i, 28)].reshape(28 * 16, 256)
                got = jnp.dot(turned, rows, preferred_element_type=F32).astype(BF16)
                got = got.reshape(8, 2, 16, 256)
                for side in range(2):
                    for half in range(2):
                        terms[side, half, :, 9 * which + 3 * i + j] = got[
                            :, side, :, 128 * half : 128 * half + 128
                        ]
            return 0

        lax.fori_loop(0, 3, step, 0)

    for j in range(3):
        mine[j, :8] = jnp.zeros((8, 16, 256), BF16)
        mine[j, 32:] = jnp.zeros((8, 16, 256), BF16)
    weight_terms(narrowed(hidden[144:816], 24, -4), second[192:768], 24, 1)
    image_band = acts[pl.ds(6 + 24 * core, 28), :W, :].reshape(28 * W, 256)
    weight_terms(narrowed(image_band, W, -6), first[8:32].reshape(24 * 16, 256), 16, 0)
    send[...] = terms[1 - core].reshape(2, 8, 288, 128)
    keep[...] = terms[core].reshape(2, 8, 288, 128)


def scatter_kernel(keep, got, image_keep, image_got, outs):
    core = lax.axis_index("core")
    for j, (y, x) in enumerate(RING):
        half, q = y // 2, 4 * (y % 2) + x
        outs[j, :288, :] = (keep[half, q].astype(F32) + got[half, q].astype(F32)).astype(BF16)
    for half in range(2):
        for k in range(4):
            near = 8 * half + 4 * core + jnp.where(core == 0, k, 3 - k)
            far = 8 * half + 4 - 4 * core + jnp.where(core == 1, k, 3 - k)
            outs[near, 288:, :] = image_keep[half, k]
            outs[far, 288:, :] = image_got[half, k]


def regroup_kernel(*rest):
    pieces, windows, columns, unpacked = rest
    unpacked[...] = pieces[:, 288:, :].astype(F32)
    total = None
    for j in range(16):
        term = pieces[j, :288, :].astype(F32)
        total = term if total is None else total + term
    total = jnp.concatenate([total, jnp.zeros((96, 128), F32)], axis=0).T
    for z in range(8):
        windows[z, 48:64, :] = total[16 * z : 16 * z + 16, :128].astype(BF16)
        windows[z, 64:80, :] = total[16 * z : 16 * z + 16, 128:256].astype(BF16)
    lane = lax.broadcasted_iota(jnp.int32, (128, 128), 1)
    rest = pltpu.roll(total[:, 256:], 96, 1)
    columns[...] = jnp.zeros((256, 128), F32)
    for i in range(3):
        for j in range(16):
            columns[10 * j : 10 * j + 10, :] = unpacked[j, 10 * i : 10 * i + 10, :]
        turned = columns[...].T
        for z in range(8):
            windows[z, 16 * i : 16 * i + 16, :] = turned[16 * z : 16 * z + 16, :128].astype(BF16)
        end = turned[:, 128:]
        if i:
            end = pltpu.roll(end, 32 * i, 1)
        rest = jnp.where((lane >= 32 * i) & (lane < 32 * i + 32), end, rest)
    for z in range(8):
        windows[z, 80:, :] = rest[16 * z : 16 * z + 16].astype(BF16)


def finish_kernel(scale, pieces, image_out, grad_one, grad_two, wide):
    total = None
    for z in range(8):
        parts = [pieces[z, k : k + 16, :].astype(F32) for k in (48, 64, 80)]
        total = parts if total is None else [t + p for t, p in zip(total, parts)]
    total[2] = pltpu.roll(total[2], 32, 1)
    total = jnp.concatenate(total, axis=1) * scale
    for out, at_lane in ((grad_one, 0), (grad_two, 144)):
        part = total if at_lane == 0 else pltpu.roll(total, 384 - at_lane, 1)
        out[...] = jnp.concatenate([part[:, :256], jnp.zeros((112, 256), F32)], axis=0).T[:144, :16]
    lane = lax.broadcasted_iota(jnp.int32, (48, 384), 1)
    wide[...] = jnp.zeros((48, 1536), F32)
    for z in range(8):
        base = 160 * z // 128 * 128
        off = 160 * z - base
        tail = pieces[z, 80:, :].astype(F32)
        tail = jnp.concatenate([tail] + [pltpu.roll(tail, 128 - 32 * i, 1) for i in (1, 2)], axis=0)
        value = jnp.concatenate(
            [pieces[z, :48, :].astype(F32), tail, jnp.zeros((48, 128), F32)], axis=1
        )
        if off:
            value = pltpu.roll(value, off, 1)
        wide[:, base : base + 384] = jnp.where(
            (lane >= off) & (lane < off + 160), value, wide[:, base : base + 384]
        )
    image_out[...] = wide[:, :1280].astype(BF16)


def exchanged(array, axes, groups=None):
    return lax.all_to_all(
        array, axes, split_axis=0, concat_axis=0, axis_index_groups=groups, tiled=True
    )


def swapped(array):
    return lax.ppermute(array, "core", [(0, 1), (1, 0)])


def local(image, filter_one, filter_two, cotangent):
    scale = 1.0 / math.sqrt(48 * 1280)
    def rows_first(a):
        return jnp.transpose(a, (1, 0, 2)).reshape(48, 1280)

    filters = [jnp.transpose(f, (1, 0, 2)).reshape(144, 16) for f in (filter_one, filter_two)]
    pieces = call(
        windows_kernel,
        shape((8, 176, 128)),
        [pltpu.VMEM((48, 1792), F32)] * 2
        + [pltpu.VMEM((48, 1280), BF16)] * 2
        + [pltpu.VMEM((144, 16), BF16)] * 2
        + [pltpu.SemaphoreType.DMA((4,))],
        [
            pltpu.with_memory_space_constraint(a, pltpu.HBM)
            for a in (rows_first(image), rows_first(cotangent), *filters)
        ],
        space=pltpu.HBM,
    )
    pieces = call(
        turn_kernel,
        shape((16, 432, 128)),
        [pltpu.VMEM((384, 128), F32), pltpu.VMEM((48, 128), F32)],
        [exchanged(pieces, "z")],
    )
    pieces = exchanged(pieces, AXES, TORUS)
    send, keep, image_send, image_keep = call(
        conv_kernel,
        [shape((2, 8, 288, 128))] * 2 + [shape((2, 4, 32, 128))] * 2,
        [
            pltpu.VMEM((64, 48, 256), BF16),
            pltpu.VMEM((18, 16, 16, 256), BF16),
            pltpu.VMEM((40, 16, 256), F32),
            pltpu.VMEM((40 * 24, 256), BF16),
            pltpu.VMEM((40 * 24, 256), BF16),
            pltpu.VMEM((40, 16, 256), BF16),
            pltpu.VMEM((3, 40, 16, 256), BF16),
            pltpu.VMEM((2, 2, 8, 18, 16, 128), BF16),
            pltpu.VMEM((24, 16, 256), F32),
            pltpu.VMEM((40, 128), F32),
        ],
        [pieces, swapped(pieces)],
        room=28,
    )
    pieces = call(
        scatter_kernel,
        shape((16, 320, 128)),
        [],
        [keep, swapped(send), image_keep, swapped(image_send)],
    )
    pieces = call(
        regroup_kernel,
        shape((8, 96, 128)),
        [pltpu.VMEM((256, 128), F32), pltpu.VMEM((16, 32, 128), F32)],
        [exchanged(pieces, AXES, TORUS)],
    )
    image_grad, *filter_grads = call(
        functools.partial(finish_kernel, scale),
        [shape((48, 1280)), shape((144, 16), F32), shape((144, 16), F32)],
        [pltpu.VMEM((48, 1536), F32)],
        [exchanged(pieces, "z")],
    )
    grad_one, grad_two = (
        jnp.transpose(g.reshape(9, 16, 16), (1, 0, 2)) for g in filter_grads
    )
    return jnp.transpose(image_grad.reshape(3, 16, 1280), (1, 0, 2)), grad_one, grad_two


def solution(mesh):
    finer = Mesh(mesh.devices.reshape(2, 8, 2, 4, 2), AXES)
    return jax.shard_map(
        local,
        mesh=finer,
        in_specs=(
            P(CHAN, STRIP, None),
            P(STRIP, None, CHAN),
            P(STRIP, None, CHAN),
            P(CHAN, STRIP, None),
        ),
        out_specs=(P(CHAN, STRIP, None), P(STRIP, None, CHAN), P(STRIP, None, CHAN)),
        check_vma=False,
    )
```

```python
import functools
import math

import jax
import jax.numpy as jnp
from jax import lax
from jax.experimental import pallas as pl
from jax.experimental.pallas import tpu as pltpu
from jax.sharding import Mesh
from jax.sharding import PartitionSpec as P

AXES = ("yh", "z", "yl", "x", "core")
CHAN = ("yh", "z")
STRIP = ("yl", "x", "core")
RING = [(y, x if y % 2 == 0 else 3 - x) for y in range(4) for x in range(4)]
TORUS = [
    [(((y // 2 * 8 + z) * 2 + y % 2) * 4 + x) * 2 + core for y, x in RING]
    for z in range(8)
    for core in range(2)
]
F32 = jnp.float32
BF16 = jnp.bfloat16

W = 32


def call(kernel, outs, scratch, args, room=10, space=pltpu.VMEM):
    return pl.pallas_call(
        kernel,
        out_shape=outs,
        in_specs=[pl.BlockSpec(memory_space=space)] * len(args),
        out_specs=jax.tree.map(lambda _: pl.BlockSpec(memory_space=pltpu.VMEM), outs),
        scratch_shapes=scratch,
        compiler_params=pltpu.CompilerParams(vmem_limit_bytes=room * 2**20),
    )(*args)


def shape(dims, kind=BF16):
    return jax.ShapeDtypeStruct(dims, kind)


def windows_kernel(*rest):
    sources, (windows, image_wide, cotangent_wide), held, arrived = (
        rest[:4],
        rest[4:7],
        rest[7:11],
        rest[11],
    )
    copies = [
        pltpu.make_async_copy(a, b, arrived.at[k]) for k, (a, b) in enumerate(zip(sources, held))
    ]
    for copy in copies:
        copy.start()
    for copy in copies:
        copy.wait()
    image, cotangent, filter_one, filter_two = held
    row = lax.broadcasted_iota(jnp.int32, (16, 16), 0)
    unit = (row == lax.broadcasted_iota(jnp.int32, (16, 16), 1)).astype(F32).astype(BF16)
    pieces = jnp.concatenate(
        [
            lax.dot_general(
                unit, f[...], (((1,), (1,)), ((), ())), preferred_element_type=F32
            )
            for f in (filter_one, filter_two)
        ]
        + [jnp.zeros((16, 96), F32)],
        axis=1,
    )
    ends = pltpu.roll(pieces[:, 256:], 88, 1)
    ends = jnp.concatenate([ends, ends, ends], axis=0)
    for wide, source in ((image_wide, image), (cotangent_wide, cotangent)):
        wide[:, :256] = jnp.zeros((48, 256), F32)
        wide[:, 1536:] = jnp.zeros((48, 256), F32)
        wide[:, 256:1536] = source[...].astype(F32)
    lane = lax.broadcasted_iota(jnp.int32, (48, 384), 1)
    for z in range(8):
        first = 256 + 160 * z - 8
        base = first // 128 * 128
        left = pltpu.roll(image_wide[:, base : base + 384], 384 - (first - base), 1)
        second = 256 + 160 * z - 4 - 176
        base = second // 128 * 128
        right = pltpu.roll(cotangent_wide[:, base : base + 512], 512 - (second - base), 1)[:, :384]
        both = jnp.where(lane < 176, left, right)
        windows[z, :48, :] = both[:, :128].astype(BF16)
        windows[z, 48:96, :] = both[:, 128:256].astype(BF16)
        windows[z, 96:144, :] = jnp.where(lane[:, :128] < 88, both[:, 256:], ends).astype(BF16)
        windows[z, 144:160, :] = pieces[:, :128].astype(BF16)
        windows[z, 160:, :] = pieces[:, 128:256].astype(BF16)


def turn_kernel(*rest):
    held, outs, turned, chunk = rest
    for i in range(3):
        parts = [held[:, k + 16 * i : k + 16 * i + 16, :].reshape(128, 128) for k in (0, 48, 96)]
        turned[...] = jnp.concatenate(parts, axis=1).astype(F32).T
        for j in range(16):
            chunk[:32, :] = turned[10 * j : 10 * j + 32, :]
            chunk[26:48, :] = turned[176 + 10 * j : 198 + 10 * j, :]
            outs[j, 48 * i : 48 * i + 48, :] = chunk[...].astype(BF16)
    parts = [held[:, k : k + 16, :].reshape(128, 128).astype(F32) for k in (144, 160, 96)]
    parts[2] = pltpu.roll(parts[2], 40, 1)
    filters = jnp.concatenate(parts, axis=1).T[:288].astype(BF16)
    for j in range(16):
        outs[j, 144:, :] = filters


def sigmoid(v):
    return 0.5 + 0.5 * jnp.tanh(0.5 * v)


def rolled(value, shift):
    shift %= value.shape[0]
    return pltpu.roll(value, shift, 0) if shift else value


def tapped(band, wide, shifts, transposed):
    total = None
    for j in range(3):
        taps = [wide[3 * i + j].reshape(256, 256) for i in range(3)]
        weights = jnp.concatenate(taps, axis=1 if transposed else 0)
        over = (((1,), (1 if transposed else 0,)), ((), ()))
        term = lax.dot_general(band, weights, over, preferred_element_type=F32)
        term = rolled(term, shifts[j])
        total = term if total is None else total + term
    return total


def silu_slope(v):
    s = sigmoid(v)
    return s * (1.0 + v * (1.0 - s))


def conv_kernel(*rest):
    own, other = rest[:2]
    send, keep, image_send, image_keep = rest[2:6]
    acts, wides, pre, hidden, second, first, mine, image_rows, packed = rest[6:]
    yh, z, yl, x, core = (lax.axis_index(a) for a in AXES)
    y = 2 * yh + yl
    acts[6:8] = jnp.zeros((2, 48, 256), BF16)
    acts[56:58] = jnp.zeros((2, 48, 256), BF16)
    for pieces, side in ((own, core), (other, 1 - core)):
        for j, (at_y, at_x) in enumerate(RING):
            half = at_y // 2
            strip = 2 * (4 * (at_y % 2) + at_x) + side
            lanes = slice(half * 128, half * 128 + 128)
            acts[pl.ds(3 * strip + 8, 3), :, lanes] = pieces[j, :144, :].reshape(3, 48, 128)
            wides[:, strip, :, lanes] = pieces[j, 144:, :].reshape(18, 16, 128)
    wide_one, wide_two = wides.at[:9], wides.at[9:]

    rows_out = 6 + 26 * core
    hidden[pl.ds(pl.multiple_of(24 * rows_out, 48), 48)] = jnp.zeros((48, 256), BF16)
    second[pl.ds(pl.multiple_of(24 * rows_out, 48), 48)] = jnp.zeros((48, 256), BF16)
    first[pl.ds(rows_out, 2)] = jnp.zeros((2, 16, 256), BF16)
    left = 160 * z + 10 * (4 * y + jnp.where(yl == 0, x, 3 - x)) - 8

    def mask(begin, columns):
        c = lax.broadcasted_iota(jnp.int32, (1, columns, 256), 1) + (left + begin)
        return ((c >= 0) & (c < 1280)).astype(F32)

    def flat(start, rows):
        return pl.ds(pl.multiple_of(start * 24, 48), rows * 24)

    mask_24, mask_16 = mask(2, 24), mask(6, 16)

    for k in range(1):
        rows = 30
        start = 8 - 6 * core + 16 * k
        band = jnp.concatenate(
            [acts[pl.ds(start + 24 * core + 2 * i - 2, rows), :W, :] for i in range(3)], axis=-1
        ).reshape(rows * W, 768)
        value = tapped(band, wide_one, (0, -2, -4), False)
        pre[pl.ds(start, rows)] = rolled(value, -4).reshape(rows, W, 256)[:, :16, :]
        value = value.reshape(rows, W, 256)[:, :24, :]
        value = value * sigmoid(value) * mask_24
        hidden[flat(start, rows)] = value.reshape(rows * 24, 256).astype(BF16)

    start = 8 - 4 * core
    band = jnp.concatenate([hidden[flat(start + 2 * i - 2, 28)] for i in range(3)], axis=-1)
    value = tapped(band, wide_two, (2, 0, -2), False).reshape(28, 24, 256)
    got = acts[pl.ds(start + 24 * core, 28), 16:, :].astype(F32)[:, 8:, :]
    value = got * silu_slope(value) * mask_24
    second[flat(start, 28)] = value.reshape(28 * 24, 256).astype(BF16)

    start = 8 - 2 * core
    band = jnp.concatenate([second[flat(start - 2 * i + 2, 26)] for i in range(3)], axis=-1)
    value = tapped(band, wide_two, (-6, -4, -2), True).reshape(26, 24, 256)[:, :16, :]
    value = value * silu_slope(pre[pl.ds(start, 26)]) * mask_16
    first[pl.ds(start, 26)] = value.astype(BF16)

    band = jnp.concatenate([first[10 - 2 * i : 34 - 2 * i] for i in range(3)], axis=-1)
    value = tapped(band.reshape(384, 768), wide_one, (-4, -2, 0), True)
    image_rows[...] = value.reshape(24, 16, 256)
    for side, out in ((1 - core, image_send), (core, image_keep)):
        for k in range(4):
            for half in range(2):
                lines = image_rows[pl.ds(6 * k + 3 * side, 3), :, 128 * half : 128 * half + 128]
                for i in range(3):
                    packed[10 * i : 10 * i + 16, :] = lines[i]
                out[half, k] = packed[:32, :].astype(BF16)

    def narrowed(values, columns, shift):
        rows = values.shape[0] // columns
        return rolled(values.astype(F32), shift).reshape(rows, columns, 256)[:, :16, :]

    def weight_terms(values, grads, columns, which):
        turned = values.reshape(28 * 16, 256).T.astype(BF16)
        column = lax.broadcasted_iota(jnp.int32, (24, 16, 256), 1)
        for j in range(3):
            kept = (column >= 2 * j) & (column < 2 * j + 10)
            shifted = narrowed(grads, columns, 2 * j - 2 - (4 if columns == 24 else 0))
            mine[j, 8:32] = jnp.where(kept, shifted, 0.0).astype(BF16)

        def step(i, _):
            for j in range(3):
                rows = mine[j, pl.ds(8 - 2 * i, 28)].reshape(28 * 16, 256)
                got = jnp.dot(turned, rows, preferred_element_type=F32)
                got = got.reshape(8, 2, 16, 256)
                sent = jnp.where(core == 0, got[:, 1], got[:, 0])
                kept = jnp.where(core == 0, got[:, 0], got[:, 1])
                for half in range(2):
                    lanes = slice(128 * half, 128 * half + 128)
                    send[half, :, 9 * which + 3 * i + j] = sent[:, :, lanes].astype(BF16)
                    keep[half, :, 9 * which + 3 * i + j] = kept[:, :, lanes].astype(BF16)
            return 0

        lax.fori_loop(0, 3, step, 0)

    for j in range(3):
        mine[j, :8] = jnp.zeros((8, 16, 256), BF16)
        mine[j, 32:] = jnp.zeros((8, 16, 256), BF16)
    weight_terms(narrowed(hidden[144:816], 24, -4), second[192:768], 24, 1)
    image_band = acts[pl.ds(6 + 24 * core, 28), :W, :].reshape(28 * W, 256)
    weight_terms(narrowed(image_band, W, -6), first[8:32].reshape(24 * 16, 256), 16, 0)


def scatter_kernel(keep, got, image_keep, image_got, outs):
    core = lax.axis_index("core")
    for j, (y, x) in enumerate(RING):
        half, q = y // 2, 4 * (y % 2) + x
        total = keep[half, q].astype(F32) + got[half, q].astype(F32)
        outs[j, :288, :] = total.reshape(288, 128).astype(BF16)
    for half in range(2):
        for k in range(4):
            near = 8 * half + 4 * core + jnp.where(core == 0, k, 3 - k)
            far = 8 * half + 4 - 4 * core + jnp.where(core == 1, k, 3 - k)
            outs[near, 288:, :] = image_keep[half, k]
            outs[far, 288:, :] = image_got[half, k]


def regroup_kernel(*rest):
    pieces, windows, columns, unpacked = rest
    unpacked[...] = pieces[:, 288:, :].astype(F32)
    total = None
    for j in range(16):
        term = pieces[j, :288, :].astype(F32)
        total = term if total is None else total + term
    total = jnp.concatenate([total, jnp.zeros((96, 128), F32)], axis=0).T
    for z in range(8):
        windows[z, 48:64, :] = total[16 * z : 16 * z + 16, :128].astype(BF16)
        windows[z, 64:80, :] = total[16 * z : 16 * z + 16, 128:256].astype(BF16)
    lane = lax.broadcasted_iota(jnp.int32, (128, 128), 1)
    rest = pltpu.roll(total[:, 256:], 96, 1)
    columns[...] = jnp.zeros((256, 128), F32)
    for i in range(3):
        for j in range(16):
            columns[10 * j : 10 * j + 10, :] = unpacked[j, 10 * i : 10 * i + 10, :]
        turned = columns[...].T
        for z in range(8):
            windows[z, 16 * i : 16 * i + 16, :] = turned[16 * z : 16 * z + 16, :128].astype(BF16)
        end = turned[:, 128:]
        if i:
            end = pltpu.roll(end, 32 * i, 1)
        rest = jnp.where((lane >= 32 * i) & (lane < 32 * i + 32), end, rest)
    for z in range(8):
        windows[z, 80:, :] = rest[16 * z : 16 * z + 16].astype(BF16)


def finish_kernel(scale, pieces, image_out, grad_one, grad_two, wide):
    total = None
    for z in range(8):
        parts = [pieces[z, k : k + 16, :].astype(F32) for k in (48, 64, 80)]
        total = parts if total is None else [t + p for t, p in zip(total, parts)]
    total[2] = pltpu.roll(total[2], 32, 1)
    total = jnp.concatenate(total, axis=1) * scale
    for out, at_lane in ((grad_one, 0), (grad_two, 144)):
        part = total if at_lane == 0 else pltpu.roll(total, 384 - at_lane, 1)
        out[...] = jnp.concatenate([part[:, :256], jnp.zeros((112, 256), F32)], axis=0).T[:144, :16]
    lane = lax.broadcasted_iota(jnp.int32, (48, 384), 1)
    wide[...] = jnp.zeros((48, 1536), F32)
    for z in range(8):
        base = 160 * z // 128 * 128
        off = 160 * z - base
        tail = pieces[z, 80:, :].astype(F32)
        tail = jnp.concatenate([tail] + [pltpu.roll(tail, 128 - 32 * i, 1) for i in (1, 2)], axis=0)
        value = jnp.concatenate(
            [pieces[z, :48, :].astype(F32), tail, jnp.zeros((48, 128), F32)], axis=1
        )
        if off:
            value = pltpu.roll(value, off, 1)
        wide[:, base : base + 384] = jnp.where(
            (lane >= off) & (lane < off + 160), value, wide[:, base : base + 384]
        )
    image_out[...] = wide[:, :1280].astype(BF16)


def exchanged(array, axes, groups=None):
    return lax.all_to_all(
        array, axes, split_axis=0, concat_axis=0, axis_index_groups=groups, tiled=True
    )


def swapped(array):
    return lax.ppermute(array, "core", [(0, 1), (1, 0)])


def local(image, filter_one, filter_two, cotangent):
    scale = 1.0 / math.sqrt(48 * 1280)
    def rows_first(a):
        return jnp.transpose(a, (1, 0, 2)).reshape(48, 1280)

    filters = [jnp.transpose(f, (1, 0, 2)).reshape(144, 16) for f in (filter_one, filter_two)]
    pieces = call(
        windows_kernel,
        shape((8, 176, 128)),
        [pltpu.VMEM((48, 1792), F32)] * 2
        + [pltpu.VMEM((48, 1280), BF16)] * 2
        + [pltpu.VMEM((144, 16), BF16)] * 2
        + [pltpu.SemaphoreType.DMA((4,))],
        [
            pltpu.with_memory_space_constraint(a, pltpu.HBM)
            for a in (rows_first(image), rows_first(cotangent), *filters)
        ],
        space=pltpu.HBM,
    )
    pieces = call(
        turn_kernel,
        shape((16, 432, 128)),
        [pltpu.VMEM((384, 128), F32), pltpu.VMEM((48, 128), F32)],
        [exchanged(pieces, "z")],
    )
    pieces = exchanged(pieces, AXES, TORUS)
    send, keep, image_send, image_keep = call(
        conv_kernel,
        [shape((2, 8, 18, 16, 128))] * 2 + [shape((2, 4, 32, 128))] * 2,
        [
            pltpu.VMEM((64, 48, 256), BF16),
            pltpu.VMEM((18, 16, 16, 256), BF16),
            pltpu.VMEM((40, 16, 256), F32),
            pltpu.VMEM((40 * 24, 256), BF16),
            pltpu.VMEM((40 * 24, 256), BF16),
            pltpu.VMEM((40, 16, 256), BF16),
            pltpu.VMEM((3, 40, 16, 256), BF16),
            pltpu.VMEM((24, 16, 256), F32),
            pltpu.VMEM((40, 128), F32),
        ],
        [pieces, swapped(pieces)],
        room=28,
    )
    pieces = call(
        scatter_kernel,
        shape((16, 320, 128)),
        [],
        [keep, swapped(send), image_keep, swapped(image_send)],
    )
    pieces = call(
        regroup_kernel,
        shape((8, 96, 128)),
        [pltpu.VMEM((256, 128), F32), pltpu.VMEM((16, 32, 128), F32)],
        [exchanged(pieces, AXES, TORUS)],
    )
    image_grad, *filter_grads = call(
        functools.partial(finish_kernel, scale),
        [shape((48, 1280)), shape((144, 16), F32), shape((144, 16), F32)],
        [pltpu.VMEM((48, 1536), F32)],
        [exchanged(pieces, "z")],
    )
    grad_one, grad_two = (
        jnp.transpose(g.reshape(9, 16, 16), (1, 0, 2)) for g in filter_grads
    )
    return jnp.transpose(image_grad.reshape(3, 16, 1280), (1, 0, 2)), grad_one, grad_two


def solution(mesh):
    finer = Mesh(mesh.devices.reshape(2, 8, 2, 4, 2), AXES)
    return jax.shard_map(
        local,
        mesh=finer,
        in_specs=(
            P(CHAN, STRIP, None),
            P(STRIP, None, CHAN),
            P(STRIP, None, CHAN),
            P(CHAN, STRIP, None),
        ),
        out_specs=(P(CHAN, STRIP, None), P(STRIP, None, CHAN), P(STRIP, None, CHAN)),
        check_vma=False,
    )
```

```python
import functools
import math

import jax
import jax.numpy as jnp
from jax import lax
from jax.experimental import pallas as pl
from jax.experimental.pallas import tpu as pltpu
from jax.sharding import Mesh
from jax.sharding import PartitionSpec as P

AXES = ("yh", "z", "yl", "x", "core")
CHAN = ("yh", "z")
STRIP = ("yl", "x", "core")
RING = [(y, x if y % 2 == 0 else 3 - x) for y in range(4) for x in range(4)]
TORUS = [
    [(((y // 2 * 8 + z) * 2 + y % 2) * 4 + x) * 2 + core for y, x in RING]
    for z in range(8)
    for core in range(2)
]
F32 = jnp.float32
BF16 = jnp.bfloat16

W = 32


def call(kernel, outs, scratch, args, room=10, space=pltpu.VMEM):
    return pl.pallas_call(
        kernel,
        out_shape=outs,
        in_specs=[pl.BlockSpec(memory_space=space)] * len(args),
        out_specs=jax.tree.map(lambda _: pl.BlockSpec(memory_space=pltpu.VMEM), outs),
        scratch_shapes=scratch,
        compiler_params=pltpu.CompilerParams(vmem_limit_bytes=room * 2**20),
    )(*args)


def shape(dims, kind=BF16):
    return jax.ShapeDtypeStruct(dims, kind)


def windows_kernel(*rest):
    sources, (windows, image_wide, cotangent_wide), held, arrived = (
        rest[:4],
        rest[4:7],
        rest[7:11],
        rest[11],
    )
    copies = [
        pltpu.make_async_copy(a, b, arrived.at[k]) for k, (a, b) in enumerate(zip(sources, held))
    ]
    for copy in copies:
        copy.start()
    for copy in copies:
        copy.wait()
    image, cotangent, filter_one, filter_two = held
    row = lax.broadcasted_iota(jnp.int32, (16, 16), 0)
    unit = (row == lax.broadcasted_iota(jnp.int32, (16, 16), 1)).astype(F32).astype(BF16)
    pieces = jnp.concatenate(
        [
            lax.dot_general(
                unit, f[...], (((1,), (1,)), ((), ())), preferred_element_type=F32
            )
            for f in (filter_one, filter_two)
        ]
        + [jnp.zeros((16, 96), F32)],
        axis=1,
    )
    ends = pltpu.roll(pieces[:, 256:], 88, 1)
    ends = jnp.concatenate([ends, ends, ends], axis=0)
    for wide, source in ((image_wide, image), (cotangent_wide, cotangent)):
        wide[:, :256] = jnp.zeros((48, 256), F32)
        wide[:, 1536:] = jnp.zeros((48, 256), F32)
        wide[:, 256:1536] = source[...].astype(F32)
    lane = lax.broadcasted_iota(jnp.int32, (48, 384), 1)
    for z in range(8):
        first = 256 + 160 * z - 8
        base = first // 128 * 128
        left = pltpu.roll(image_wide[:, base : base + 384], 384 - (first - base), 1)
        second = 256 + 160 * z - 4 - 176
        base = second // 128 * 128
        right = pltpu.roll(cotangent_wide[:, base : base + 512], 512 - (second - base), 1)[:, :384]
        both = jnp.where(lane < 176, left, right)
        windows[z, :48, :] = both[:, :128].astype(BF16)
        windows[z, 48:96, :] = both[:, 128:256].astype(BF16)
        windows[z, 96:144, :] = jnp.where(lane[:, :128] < 88, both[:, 256:], ends).astype(BF16)
        windows[z, 144:160, :] = pieces[:, :128].astype(BF16)
        windows[z, 160:, :] = pieces[:, 128:256].astype(BF16)


def turn_kernel(*rest):
    held, outs, turned, chunk = rest
    for i in range(3):
        parts = [held[:, k + 16 * i : k + 16 * i + 16, :].reshape(128, 128) for k in (0, 48, 96)]
        turned[...] = jnp.concatenate(parts, axis=1).astype(F32).T
        for j in range(16):
            chunk[:32, :] = turned[10 * j : 10 * j + 32, :]
            chunk[26:48, :] = turned[176 + 10 * j : 198 + 10 * j, :]
            outs[j, 48 * i : 48 * i + 48, :] = chunk[...].astype(BF16)
    parts = [held[:, k : k + 16, :].reshape(128, 128).astype(F32) for k in (144, 160, 96)]
    parts[2] = pltpu.roll(parts[2], 40, 1)
    filters = jnp.concatenate(parts, axis=1).T[:288].astype(BF16)
    for j in range(16):
        outs[j, 144:, :] = filters


def sigmoid(v):
    return 0.5 + 0.5 * jnp.tanh(0.5 * v)


def rolled(value, shift):
    shift %= value.shape[0]
    return pltpu.roll(value, shift, 0) if shift else value


def tapped(band, wide, shifts, transposed):
    total = None
    for j in range(3):
        taps = [wide[3 * i + j].reshape(256, 256) for i in range(3)]
        weights = jnp.concatenate(taps, axis=1 if transposed else 0)
        over = (((1,), (1 if transposed else 0,)), ((), ()))
        term = lax.dot_general(band, weights, over, preferred_element_type=F32)
        term = rolled(term, shifts[j])
        total = term if total is None else total + term
    return total


def silu_slope(v):
    s = sigmoid(v)
    return s * (1.0 + v * (1.0 - s))


def conv_kernel(*rest):
    own, other = rest[:2]
    send, keep = rest[2:4]
    acts, wides, pre, hidden, second, first, mine, image_rows, packed = rest[4:]
    yh, z, yl, x, core = (lax.axis_index(a) for a in AXES)
    y = 2 * yh + yl
    acts[6:8] = jnp.zeros((2, 48, 256), BF16)
    acts[56:58] = jnp.zeros((2, 48, 256), BF16)
    for pieces, side in ((own, core), (other, 1 - core)):
        for j, (at_y, at_x) in enumerate(RING):
            half = at_y // 2
            strip = 2 * (4 * (at_y % 2) + at_x) + side
            lanes = slice(half * 128, half * 128 + 128)
            acts[pl.ds(3 * strip + 8, 3), :, lanes] = pieces[j, :144, :].reshape(3, 48, 128)
            wides[:, strip, :, lanes] = pieces[j, 144:, :].reshape(18, 16, 128)
    wide_one, wide_two = wides.at[:9], wides.at[9:]

    rows_out = 6 + 26 * core
    hidden[pl.ds(pl.multiple_of(24 * rows_out, 48), 48)] = jnp.zeros((48, 256), BF16)
    second[pl.ds(pl.multiple_of(24 * rows_out, 48), 48)] = jnp.zeros((48, 256), BF16)
    first[pl.ds(rows_out, 2)] = jnp.zeros((2, 16, 256), BF16)
    left = 160 * z + 10 * (4 * y + jnp.where(yl == 0, x, 3 - x)) - 8

    def mask(begin, columns):
        c = lax.broadcasted_iota(jnp.int32, (1, columns, 256), 1) + (left + begin)
        return ((c >= 0) & (c < 1280)).astype(F32)

    def flat(start, rows):
        return pl.ds(pl.multiple_of(start * 24, 48), rows * 24)

    mask_24, mask_16 = mask(2, 24), mask(6, 16)

    for k in range(1):
        rows = 30
        start = 8 - 6 * core + 16 * k
        band = jnp.concatenate(
            [acts[pl.ds(start + 24 * core + 2 * i - 2, rows), :W, :] for i in range(3)], axis=-1
        ).reshape(rows * W, 768)
        value = tapped(band, wide_one, (0, -2, -4), False)
        pre[pl.ds(start, rows)] = rolled(value, -4).reshape(rows, W, 256)[:, :16, :]
        value = value.reshape(rows, W, 256)[:, :24, :]
        value = value * sigmoid(value) * mask_24
        hidden[flat(start, rows)] = value.reshape(rows * 24, 256).astype(BF16)

    start = 8 - 4 * core
    band = jnp.concatenate([hidden[flat(start + 2 * i - 2, 28)] for i in range(3)], axis=-1)
    value = tapped(band, wide_two, (2, 0, -2), False).reshape(28, 24, 256)
    got = acts[pl.ds(start + 24 * core, 28), 16:, :].astype(F32)[:, 8:, :]
    value = got * silu_slope(value) * mask_24
    second[flat(start, 28)] = value.reshape(28 * 24, 256).astype(BF16)

    start = 8 - 2 * core
    band = jnp.concatenate([second[flat(start - 2 * i + 2, 26)] for i in range(3)], axis=-1)
    value = tapped(band, wide_two, (-6, -4, -2), True).reshape(26, 24, 256)[:, :16, :]
    value = value * silu_slope(pre[pl.ds(start, 26)]) * mask_16
    first[pl.ds(start, 26)] = value.astype(BF16)

    band = jnp.concatenate([first[10 - 2 * i : 34 - 2 * i] for i in range(3)], axis=-1)
    value = tapped(band.reshape(384, 768), wide_one, (-4, -2, 0), True)
    image_rows[...] = value.reshape(24, 16, 256)
    for side, out in ((1 - core, send), (core, keep)):
        for k in range(4):
            for half in range(2):
                lines = image_rows[pl.ds(6 * k + 3 * side, 3), :, 128 * half : 128 * half + 128]
                for i in range(3):
                    packed[10 * i : 10 * i + 16, :] = lines[i]
                out[half, 144 + 2 * k : 146 + 2 * k] = (
                    packed[:32, :].astype(BF16).reshape(2, 16, 128)
                )

    def narrowed(values, columns, shift):
        rows = values.shape[0] // columns
        return rolled(values.astype(F32), shift).reshape(rows, columns, 256)[:, :16, :]

    def weight_terms(values, grads, columns, which):
        turned = values.reshape(28 * 16, 256).T.astype(BF16)
        column = lax.broadcasted_iota(jnp.int32, (24, 16, 256), 1)
        for j in range(3):
            kept = (column >= 2 * j) & (column < 2 * j + 10)
            shifted = narrowed(grads, columns, 2 * j - 2 - (4 if columns == 24 else 0))
            mine[j, 8:32] = jnp.where(kept, shifted, 0.0).astype(BF16)

        def step(i, _):
            for j in range(3):
                rows = mine[j, pl.ds(8 - 2 * i, 28)].reshape(28 * 16, 256)
                got = jnp.dot(turned, rows, preferred_element_type=F32)
                got = got.reshape(8, 2, 16, 256)
                sent = jnp.where(core == 0, got[:, 1], got[:, 0])
                kept = jnp.where(core == 0, got[:, 0], got[:, 1])
                for half in range(2):
                    lanes = slice(128 * half, 128 * half + 128)
                    for q in range(8):
                        place = 18 * q + 9 * which + 3 * i + j
                        send[half, place] = sent[q, :, lanes].astype(BF16)
                        keep[half, place] = kept[q, :, lanes].astype(BF16)
            return 0

        lax.fori_loop(0, 3, step, 0)

    for j in range(3):
        mine[j, :8] = jnp.zeros((8, 16, 256), BF16)
        mine[j, 32:] = jnp.zeros((8, 16, 256), BF16)
    weight_terms(narrowed(hidden[144:816], 24, -4), second[192:768], 24, 1)
    image_band = acts[pl.ds(6 + 24 * core, 28), :W, :].reshape(28 * W, 256)
    weight_terms(narrowed(image_band, W, -6), first[8:32].reshape(24 * 16, 256), 16, 0)


def scatter_kernel(keep, got, outs):
    core = lax.axis_index("core")
    for j, (y, x) in enumerate(RING):
        half, q = y // 2, 4 * (y % 2) + x
        part = slice(18 * q, 18 * q + 18)
        total = keep[half, part].astype(F32) + got[half, part].astype(F32)
        outs[j, :288, :] = total.reshape(288, 128).astype(BF16)
    for half in range(2):
        for k in range(4):
            near = 8 * half + 4 * core + jnp.where(core == 0, k, 3 - k)
            far = 8 * half + 4 - 4 * core + jnp.where(core == 1, k, 3 - k)
            part = slice(144 + 2 * k, 146 + 2 * k)
            outs[near, 288:, :] = keep[half, part].reshape(32, 128)
            outs[far, 288:, :] = got[half, part].reshape(32, 128)


def regroup_kernel(*rest):
    pieces, windows, columns, unpacked = rest
    unpacked[...] = pieces[:, 288:, :].astype(F32)
    total = None
    for j in range(16):
        term = pieces[j, :288, :].astype(F32)
        total = term if total is None else total + term
    total = jnp.concatenate([total, jnp.zeros((96, 128), F32)], axis=0).T
    for z in range(8):
        windows[z, 48:64, :] = total[16 * z : 16 * z + 16, :128].astype(BF16)
        windows[z, 64:80, :] = total[16 * z : 16 * z + 16, 128:256].astype(BF16)
    lane = lax.broadcasted_iota(jnp.int32, (128, 128), 1)
    rest = pltpu.roll(total[:, 256:], 96, 1)
    columns[...] = jnp.zeros((256, 128), F32)
    for i in range(3):
        for j in range(16):
            columns[10 * j : 10 * j + 10, :] = unpacked[j, 10 * i : 10 * i + 10, :]
        turned = columns[...].T
        for z in range(8):
            windows[z, 16 * i : 16 * i + 16, :] = turned[16 * z : 16 * z + 16, :128].astype(BF16)
        end = turned[:, 128:]
        if i:
            end = pltpu.roll(end, 32 * i, 1)
        rest = jnp.where((lane >= 32 * i) & (lane < 32 * i + 32), end, rest)
    for z in range(8):
        windows[z, 80:, :] = rest[16 * z : 16 * z + 16].astype(BF16)


def finish_kernel(scale, pieces, image_out, grad_one, grad_two, wide):
    total = None
    for z in range(8):
        parts = [pieces[z, k : k + 16, :].astype(F32) for k in (48, 64, 80)]
        total = parts if total is None else [t + p for t, p in zip(total, parts)]
    total[2] = pltpu.roll(total[2], 32, 1)
    total = jnp.concatenate(total, axis=1) * scale
    for out, at_lane in ((grad_one, 0), (grad_two, 144)):
        part = total if at_lane == 0 else pltpu.roll(total, 384 - at_lane, 1)
        out[...] = jnp.concatenate([part[:, :256], jnp.zeros((112, 256), F32)], axis=0).T[:144, :16]
    lane = lax.broadcasted_iota(jnp.int32, (48, 384), 1)
    wide[...] = jnp.zeros((48, 1536), F32)
    for z in range(8):
        base = 160 * z // 128 * 128
        off = 160 * z - base
        tail = pieces[z, 80:, :].astype(F32)
        tail = jnp.concatenate([tail] + [pltpu.roll(tail, 128 - 32 * i, 1) for i in (1, 2)], axis=0)
        value = jnp.concatenate(
            [pieces[z, :48, :].astype(F32), tail, jnp.zeros((48, 128), F32)], axis=1
        )
        if off:
            value = pltpu.roll(value, off, 1)
        wide[:, base : base + 384] = jnp.where(
            (lane >= off) & (lane < off + 160), value, wide[:, base : base + 384]
        )
    image_out[...] = wide[:, :1280].astype(BF16)


def exchanged(array, axes, groups=None):
    return lax.all_to_all(
        array, axes, split_axis=0, concat_axis=0, axis_index_groups=groups, tiled=True
    )


def swapped(array):
    return lax.ppermute(array, "core", [(0, 1), (1, 0)])


def local(image, filter_one, filter_two, cotangent):
    scale = 1.0 / math.sqrt(48 * 1280)
    def rows_first(a):
        return jnp.transpose(a, (1, 0, 2)).reshape(48, 1280)

    filters = [jnp.transpose(f, (1, 0, 2)).reshape(144, 16) for f in (filter_one, filter_two)]
    pieces = call(
        windows_kernel,
        shape((8, 176, 128)),
        [pltpu.VMEM((48, 1792), F32)] * 2
        + [pltpu.VMEM((48, 1280), BF16)] * 2
        + [pltpu.VMEM((144, 16), BF16)] * 2
        + [pltpu.SemaphoreType.DMA((4,))],
        [
            pltpu.with_memory_space_constraint(a, pltpu.HBM)
            for a in (rows_first(image), rows_first(cotangent), *filters)
        ],
        space=pltpu.HBM,
    )
    pieces = call(
        turn_kernel,
        shape((16, 432, 128)),
        [pltpu.VMEM((384, 128), F32), pltpu.VMEM((48, 128), F32)],
        [exchanged(pieces, "z")],
    )
    pieces = exchanged(pieces, AXES, TORUS)
    send, keep = call(
        conv_kernel,
        [shape((2, 152, 16, 128))] * 2,
        [
            pltpu.VMEM((64, 48, 256), BF16),
            pltpu.VMEM((18, 16, 16, 256), BF16),
            pltpu.VMEM((40, 16, 256), F32),
            pltpu.VMEM((40 * 24, 256), BF16),
            pltpu.VMEM((40 * 24, 256), BF16),
            pltpu.VMEM((40, 16, 256), BF16),
            pltpu.VMEM((3, 40, 16, 256), BF16),
            pltpu.VMEM((24, 16, 256), F32),
            pltpu.VMEM((40, 128), F32),
        ],
        [pieces, swapped(pieces)],
        room=28,
    )
    pieces = call(
        scatter_kernel,
        shape((16, 320, 128)),
        [],
        [keep, swapped(send)],
    )
    pieces = call(
        regroup_kernel,
        shape((8, 96, 128)),
        [pltpu.VMEM((256, 128), F32), pltpu.VMEM((16, 32, 128), F32)],
        [exchanged(pieces, AXES, TORUS)],
    )
    image_grad, *filter_grads = call(
        functools.partial(finish_kernel, scale),
        [shape((48, 1280)), shape((144, 16), F32), shape((144, 16), F32)],
        [pltpu.VMEM((48, 1536), F32)],
        [exchanged(pieces, "z")],
    )
    grad_one, grad_two = (
        jnp.transpose(g.reshape(9, 16, 16), (1, 0, 2)) for g in filter_grads
    )
    return jnp.transpose(image_grad.reshape(3, 16, 1280), (1, 0, 2)), grad_one, grad_two


def solution(mesh):
    finer = Mesh(mesh.devices.reshape(2, 8, 2, 4, 2), AXES)
    return jax.shard_map(
        local,
        mesh=finer,
        in_specs=(
            P(CHAN, STRIP, None),
            P(STRIP, None, CHAN),
            P(STRIP, None, CHAN),
            P(CHAN, STRIP, None),
        ),
        out_specs=(P(CHAN, STRIP, None), P(STRIP, None, CHAN), P(STRIP, None, CHAN)),
        check_vma=False,
    )
```

```python
import functools
import math

import jax
import jax.numpy as jnp
from jax import lax
from jax.experimental import pallas as pl
from jax.experimental.pallas import tpu as pltpu
from jax.sharding import Mesh
from jax.sharding import PartitionSpec as P

AXES = ("yh", "z", "yl", "x", "core")
CHAN = ("yh", "z")
STRIP = ("yl", "x", "core")
RING = [(y, x if y % 2 == 0 else 3 - x) for y in range(4) for x in range(4)]
TORUS = [
    [(((y // 2 * 8 + z) * 2 + y % 2) * 4 + x) * 2 + core for y, x in RING]
    for z in range(8)
    for core in range(2)
]
F32 = jnp.float32
BF16 = jnp.bfloat16

W = 32


def call(kernel, outs, scratch, args, room=10, space=pltpu.VMEM):
    return pl.pallas_call(
        kernel,
        out_shape=outs,
        in_specs=[pl.BlockSpec(memory_space=space)] * len(args),
        out_specs=jax.tree.map(lambda _: pl.BlockSpec(memory_space=pltpu.VMEM), outs),
        scratch_shapes=scratch,
        compiler_params=pltpu.CompilerParams(vmem_limit_bytes=room * 2**20),
    )(*args)


def shape(dims, kind=BF16):
    return jax.ShapeDtypeStruct(dims, kind)


def windows_kernel(*rest):
    sources, (windows, image_wide, cotangent_wide), held, arrived = (
        rest[:4],
        rest[4:7],
        rest[7:11],
        rest[11],
    )
    copies = [
        pltpu.make_async_copy(a, b, arrived.at[k]) for k, (a, b) in enumerate(zip(sources, held))
    ]
    for copy in copies:
        copy.start()
    for copy in copies:
        copy.wait()
    image, cotangent, filter_one, filter_two = held
    row = lax.broadcasted_iota(jnp.int32, (16, 16), 0)
    unit = (row == lax.broadcasted_iota(jnp.int32, (16, 16), 1)).astype(F32).astype(BF16)
    pieces = jnp.concatenate(
        [
            lax.dot_general(
                unit, f[...], (((1,), (1,)), ((), ())), preferred_element_type=F32
            )
            for f in (filter_one, filter_two)
        ]
        + [jnp.zeros((16, 96), F32)],
        axis=1,
    )
    ends = pltpu.roll(pieces[:, 256:], 88, 1)
    ends = jnp.concatenate([ends, ends, ends], axis=0)
    for wide, source in ((image_wide, image), (cotangent_wide, cotangent)):
        wide[:, :256] = jnp.zeros((48, 256), F32)
        wide[:, 1536:] = jnp.zeros((48, 256), F32)
        wide[:, 256:1536] = source[...].astype(F32)
    lane = lax.broadcasted_iota(jnp.int32, (48, 384), 1)
    for z in range(8):
        first = 256 + 160 * z - 8
        base = first // 128 * 128
        left = pltpu.roll(image_wide[:, base : base + 384], 384 - (first - base), 1)
        second = 256 + 160 * z - 4 - 176
        base = second // 128 * 128
        right = pltpu.roll(cotangent_wide[:, base : base + 512], 512 - (second - base), 1)[:, :384]
        both = jnp.where(lane < 176, left, right)
        windows[z, :48, :] = both[:, :128].astype(BF16)
        windows[z, 48:96, :] = both[:, 128:256].astype(BF16)
        windows[z, 96:144, :] = jnp.where(lane[:, :128] < 88, both[:, 256:], ends).astype(BF16)
        windows[z, 144:160, :] = pieces[:, :128].astype(BF16)
        windows[z, 160:, :] = pieces[:, 128:256].astype(BF16)


def turn_kernel(*rest):
    held, outs, turned, chunk = rest
    for i in range(3):
        parts = [held[:, k + 16 * i : k + 16 * i + 16, :].reshape(128, 128) for k in (0, 48, 96)]
        turned[...] = jnp.concatenate(parts, axis=1).astype(F32).T
        for j in range(16):
            chunk[:32, :] = turned[10 * j : 10 * j + 32, :]
            chunk[26:48, :] = turned[176 + 10 * j : 198 + 10 * j, :]
            outs[j, 48 * i : 48 * i + 48, :] = chunk[...].astype(BF16)
    parts = [held[:, k : k + 16, :].reshape(128, 128).astype(F32) for k in (144, 160, 96)]
    parts[2] = pltpu.roll(parts[2], 40, 1)
    filters = jnp.concatenate(parts, axis=1).T[:288].astype(BF16)
    for j in range(16):
        outs[j, 144:, :] = filters


def sigmoid(v):
    return 0.5 + 0.5 * jnp.tanh(0.5 * v)


def rolled(value, shift):
    shift %= value.shape[0]
    return pltpu.roll(value, shift, 0) if shift else value


def tapped(band, wide, shifts, transposed):
    total = None
    for j in range(3):
        taps = [wide[3 * i + j].reshape(256, 256) for i in range(3)]
        weights = jnp.concatenate(taps, axis=1 if transposed else 0)
        over = (((1,), (1 if transposed else 0,)), ((), ()))
        term = lax.dot_general(band, weights, over, preferred_element_type=F32)
        term = rolled(term, shifts[j])
        total = term if total is None else total + term
    return total


def silu_slope(v):
    s = sigmoid(v)
    return s * (1.0 + v * (1.0 - s))


def conv_kernel(*rest):
    own, other = rest[:2]
    send, keep, image_send, image_keep = rest[2:6]
    acts, wides, pre, hidden, second, first, mine, image_rows, packed = rest[6:]
    yh, z, yl, x, core = (lax.axis_index(a) for a in AXES)
    y = 2 * yh + yl
    acts[6:8] = jnp.zeros((2, 48, 256), BF16)
    acts[56:58] = jnp.zeros((2, 48, 256), BF16)
    for pieces, side in ((own, core), (other, 1 - core)):
        for j, (at_y, at_x) in enumerate(RING):
            half = at_y // 2
            strip = 2 * (4 * (at_y % 2) + at_x) + side
            lanes = slice(half * 128, half * 128 + 128)
            acts[pl.ds(3 * strip + 8, 3), :, lanes] = pieces[j, :144, :].reshape(3, 48, 128)
            wides[:, strip, :, lanes] = pieces[j, 144:, :].reshape(18, 16, 128)
    wide_one, wide_two = wides.at[:9], wides.at[9:]

    rows_out = 6 + 26 * core
    hidden[pl.ds(pl.multiple_of(24 * rows_out, 48), 48)] = jnp.zeros((48, 256), BF16)
    second[pl.ds(pl.multiple_of(24 * rows_out, 48), 48)] = jnp.zeros((48, 256), BF16)
    first[pl.ds(rows_out, 2)] = jnp.zeros((2, 16, 256), BF16)
    left = 160 * z + 10 * (4 * y + jnp.where(yl == 0, x, 3 - x)) - 8

    def mask(begin, columns):
        c = lax.broadcasted_iota(jnp.int32, (1, columns, 256), 1) + (left + begin)
        return ((c >= 0) & (c < 1280)).astype(F32)

    def flat(start, rows):
        return pl.ds(pl.multiple_of(start * 24, 48), rows * 24)

    mask_24, mask_16 = mask(2, 24), mask(6, 16)

    for k in range(1):
        rows = 30
        start = 8 - 6 * core + 16 * k
        band = jnp.concatenate(
            [acts[pl.ds(start + 24 * core + 2 * i - 2, rows), :W, :] for i in range(3)], axis=-1
        ).reshape(rows * W, 768)
        value = tapped(band, wide_one, (0, -2, -4), False)
        pre[pl.ds(start, rows)] = rolled(value, -4).reshape(rows, W, 256)[:, :16, :]
        value = value.reshape(rows, W, 256)[:, :24, :]
        value = value * sigmoid(value) * mask_24
        hidden[flat(start, rows)] = value.reshape(rows * 24, 256).astype(BF16)

    start = 8 - 4 * core
    band = jnp.concatenate([hidden[flat(start + 2 * i - 2, 28)] for i in range(3)], axis=-1)
    value = tapped(band, wide_two, (2, 0, -2), False).reshape(28, 24, 256)
    got = acts[pl.ds(start + 24 * core, 28), 16:, :].astype(F32)[:, 8:, :]
    value = got * silu_slope(value) * mask_24
    second[flat(start, 28)] = value.reshape(28 * 24, 256).astype(BF16)

    start = 8 - 2 * core
    band = jnp.concatenate([second[flat(start - 2 * i + 2, 26)] for i in range(3)], axis=-1)
    value = tapped(band, wide_two, (-6, -4, -2), True).reshape(26, 24, 256)[:, :16, :]
    value = value * silu_slope(pre[pl.ds(start, 26)]) * mask_16
    first[pl.ds(start, 26)] = value.astype(BF16)

    band = jnp.concatenate([first[10 - 2 * i : 34 - 2 * i] for i in range(3)], axis=-1)
    value = tapped(band.reshape(384, 768), wide_one, (-4, -2, 0), True)
    image_rows[...] = value.reshape(24, 16, 256)
    for side, out in ((1 - core, image_send), (core, image_keep)):
        for k in range(4):
            for half in range(2):
                lines = image_rows[pl.ds(6 * k + 3 * side, 3), :, 128 * half : 128 * half + 128]
                for i in range(3):
                    packed[10 * i : 10 * i + 16, :] = lines[i]
                out[half, k] = packed[:32, :].astype(BF16)

    def narrowed(values, columns, shift):
        rows = values.shape[0] // columns
        return rolled(values.astype(F32), shift).reshape(rows, columns, 256)[:, :16, :]

    def weight_terms(values, grads, columns, which):
        turned = values.reshape(28 * 16, 256).T.astype(BF16)
        column = lax.broadcasted_iota(jnp.int32, (24, 16, 256), 1)
        for j in range(3):
            kept = (column >= 2 * j) & (column < 2 * j + 10)
            shifted = narrowed(grads, columns, 2 * j - 2 - (4 if columns == 24 else 0))
            mine[j, 8:32] = jnp.where(kept, shifted, 0.0).astype(BF16)

        def step(i, _):
            rows = [mine[j, pl.ds(8 - 2 * i, 28)].reshape(28 * 16, 256) for j in range(3)]
            every = jnp.dot(turned, jnp.concatenate(rows, axis=1), preferred_element_type=F32)
            for j in range(3):
                got = every[:, 256 * j : 256 * j + 256].reshape(8, 2, 16, 256)
                sent = jnp.where(core == 0, got[:, 1], got[:, 0])
                kept = jnp.where(core == 0, got[:, 0], got[:, 1])
                for half in range(2):
                    lanes = slice(128 * half, 128 * half + 128)
                    send[half, :, 9 * which + 3 * i + j] = sent[:, :, lanes].astype(BF16)
                    keep[half, :, 9 * which + 3 * i + j] = kept[:, :, lanes].astype(BF16)
            return 0

        lax.fori_loop(0, 3, step, 0)

    for j in range(3):
        mine[j, :8] = jnp.zeros((8, 16, 256), BF16)
        mine[j, 32:] = jnp.zeros((8, 16, 256), BF16)
    weight_terms(narrowed(hidden[144:816], 24, -4), second[192:768], 24, 1)
    image_band = acts[pl.ds(6 + 24 * core, 28), :W, :].reshape(28 * W, 256)
    weight_terms(narrowed(image_band, W, -6), first[8:32].reshape(24 * 16, 256), 16, 0)


def scatter_kernel(keep, got, image_keep, image_got, outs):
    core = lax.axis_index("core")
    for j, (y, x) in enumerate(RING):
        half, q = y // 2, 4 * (y % 2) + x
        total = keep[half, q].astype(F32) + got[half, q].astype(F32)
        outs[j, :288, :] = total.reshape(288, 128).astype(BF16)
    for half in range(2):
        for k in range(4):
            near = 8 * half + 4 * core + jnp.where(core == 0, k, 3 - k)
            far = 8 * half + 4 - 4 * core + jnp.where(core == 1, k, 3 - k)
            outs[near, 288:, :] = image_keep[half, k]
            outs[far, 288:, :] = image_got[half, k]


def regroup_kernel(*rest):
    pieces, windows, columns, unpacked = rest
    unpacked[...] = pieces[:, 288:, :].astype(F32)
    total = None
    for j in range(16):
        term = pieces[j, :288, :].astype(F32)
        total = term if total is None else total + term
    total = jnp.concatenate([total, jnp.zeros((96, 128), F32)], axis=0).T
    for z in range(8):
        windows[z, 48:64, :] = total[16 * z : 16 * z + 16, :128].astype(BF16)
        windows[z, 64:80, :] = total[16 * z : 16 * z + 16, 128:256].astype(BF16)
    lane = lax.broadcasted_iota(jnp.int32, (128, 128), 1)
    rest = pltpu.roll(total[:, 256:], 96, 1)
    columns[...] = jnp.zeros((256, 128), F32)
    for i in range(3):
        for j in range(16):
            columns[10 * j : 10 * j + 10, :] = unpacked[j, 10 * i : 10 * i + 10, :]
        turned = columns[...].T
        for z in range(8):
            windows[z, 16 * i : 16 * i + 16, :] = turned[16 * z : 16 * z + 16, :128].astype(BF16)
        end = turned[:, 128:]
        if i:
            end = pltpu.roll(end, 32 * i, 1)
        rest = jnp.where((lane >= 32 * i) & (lane < 32 * i + 32), end, rest)
    for z in range(8):
        windows[z, 80:, :] = rest[16 * z : 16 * z + 16].astype(BF16)


def finish_kernel(scale, pieces, image_out, grad_one, grad_two, wide):
    total = None
    for z in range(8):
        parts = [pieces[z, k : k + 16, :].astype(F32) for k in (48, 64, 80)]
        total = parts if total is None else [t + p for t, p in zip(total, parts)]
    total[2] = pltpu.roll(total[2], 32, 1)
    total = jnp.concatenate(total, axis=1) * scale
    for out, at_lane in ((grad_one, 0), (grad_two, 144)):
        part = total if at_lane == 0 else pltpu.roll(total, 384 - at_lane, 1)
        out[...] = jnp.concatenate([part[:, :256], jnp.zeros((112, 256), F32)], axis=0).T[:144, :16]
    lane = lax.broadcasted_iota(jnp.int32, (48, 384), 1)
    wide[...] = jnp.zeros((48, 1536), F32)
    for z in range(8):
        base = 160 * z // 128 * 128
        off = 160 * z - base
        tail = pieces[z, 80:, :].astype(F32)
        tail = jnp.concatenate([tail] + [pltpu.roll(tail, 128 - 32 * i, 1) for i in (1, 2)], axis=0)
        value = jnp.concatenate(
            [pieces[z, :48, :].astype(F32), tail, jnp.zeros((48, 128), F32)], axis=1
        )
        if off:
            value = pltpu.roll(value, off, 1)
        wide[:, base : base + 384] = jnp.where(
            (lane >= off) & (lane < off + 160), value, wide[:, base : base + 384]
        )
    image_out[...] = wide[:, :1280].astype(BF16)


def exchanged(array, axes, groups=None):
    return lax.all_to_all(
        array, axes, split_axis=0, concat_axis=0, axis_index_groups=groups, tiled=True
    )


def swapped(array):
    return lax.ppermute(array, "core", [(0, 1), (1, 0)])


def local(image, filter_one, filter_two, cotangent):
    scale = 1.0 / math.sqrt(48 * 1280)
    def rows_first(a):
        return jnp.transpose(a, (1, 0, 2)).reshape(48, 1280)

    filters = [jnp.transpose(f, (1, 0, 2)).reshape(144, 16) for f in (filter_one, filter_two)]
    pieces = call(
        windows_kernel,
        shape((8, 176, 128)),
        [pltpu.VMEM((48, 1792), F32)] * 2
        + [pltpu.VMEM((48, 1280), BF16)] * 2
        + [pltpu.VMEM((144, 16), BF16)] * 2
        + [pltpu.SemaphoreType.DMA((4,))],
        [
            pltpu.with_memory_space_constraint(a, pltpu.HBM)
            for a in (rows_first(image), rows_first(cotangent), *filters)
        ],
        space=pltpu.HBM,
    )
    pieces = call(
        turn_kernel,
        shape((16, 432, 128)),
        [pltpu.VMEM((384, 128), F32), pltpu.VMEM((48, 128), F32)],
        [exchanged(pieces, "z")],
    )
    pieces = exchanged(pieces, AXES, TORUS)
    send, keep, image_send, image_keep = call(
        conv_kernel,
        [shape((2, 8, 18, 16, 128))] * 2 + [shape((2, 4, 32, 128))] * 2,
        [
            pltpu.VMEM((64, 48, 256), BF16),
            pltpu.VMEM((18, 16, 16, 256), BF16),
            pltpu.VMEM((40, 16, 256), F32),
            pltpu.VMEM((40 * 24, 256), BF16),
            pltpu.VMEM((40 * 24, 256), BF16),
            pltpu.VMEM((40, 16, 256), BF16),
            pltpu.VMEM((3, 40, 16, 256), BF16),
            pltpu.VMEM((24, 16, 256), F32),
            pltpu.VMEM((40, 128), F32),
        ],
        [pieces, swapped(pieces)],
        room=28,
    )
    pieces = call(
        scatter_kernel,
        shape((16, 320, 128)),
        [],
        [keep, swapped(send), image_keep, swapped(image_send)],
    )
    pieces = call(
        regroup_kernel,
        shape((8, 96, 128)),
        [pltpu.VMEM((256, 128), F32), pltpu.VMEM((16, 32, 128), F32)],
        [exchanged(pieces, AXES, TORUS)],
    )
    image_grad, *filter_grads = call(
        functools.partial(finish_kernel, scale),
        [shape((48, 1280)), shape((144, 16), F32), shape((144, 16), F32)],
        [pltpu.VMEM((48, 1536), F32)],
        [exchanged(pieces, "z")],
    )
    grad_one, grad_two = (
        jnp.transpose(g.reshape(9, 16, 16), (1, 0, 2)) for g in filter_grads
    )
    return jnp.transpose(image_grad.reshape(3, 16, 1280), (1, 0, 2)), grad_one, grad_two


def solution(mesh):
    finer = Mesh(mesh.devices.reshape(2, 8, 2, 4, 2), AXES)
    return jax.shard_map(
        local,
        mesh=finer,
        in_specs=(
            P(CHAN, STRIP, None),
            P(STRIP, None, CHAN),
            P(STRIP, None, CHAN),
            P(CHAN, STRIP, None),
        ),
        out_specs=(P(CHAN, STRIP, None), P(STRIP, None, CHAN), P(STRIP, None, CHAN)),
        check_vma=False,
    )
```
